32 devices in a mesh: lat: 8 (over z, core), lon: 4 (over y, x).
Axes of the slice: x: 2, y: 2, z: 4, core: 2. Of those that a mesh axis runs over, the one named last changes fastest.
Arguments:
- fields: float32 [6, 32, 128, 2880], P(None, None, 'lat', 'lon'), may hold values from -6 to 6
- inv_cos: float32 [128], P('lat'), may hold values from 0.9 to 8.8
- coupling_lon: float32 [6, 6], replicated, may hold values from -0.4 to 0.4
- coupling_lat: float32 [6, 6], replicated, may hold values from -1.5 to 1.5
- polar_rows: int32 [56], replicated, may hold values from 0 to 127, as said below
- bands: int32 [56], replicated, may hold values from 32 to 1024, as said below
Outputs:
- smoothed_fields: float32 [6, 32, 128, 2880], P(None, None, 'lat', 'lon')
The draws below stay inside these ranges and needn't reach their ends.
Inputs may be any that keep to these rules, and one draw needn't show every extreme that they name: `polar_rows`: ascending and distinct; each of the first 2 and the last 2 blocks of 16 rows holds exactly 14 of them, rows 0 and 127 are always listed, and no other row is listed. `bands`: the band width of the row at the same position of polar_rows: with d the row's distance from its nearest end row (0 or 127) and e the largest such distance among the listed rows at that end, it is 32 + ((992) d) // e.
All inputs are finite; a program needn't handle non-finite values.
Results may differ from the reference program's by a relative error of at most 0.00005.
Values sent between devices are 32-bit elements; how exact they have to be, the bound alone decides.
No kernel may reach another device: no remote copies, remote signals or barrier semaphores. Data moves between devices by JAX's collectives and lax.ppermute only.
A program may use at most 128 MiB of HBM per device.

```python
import math
import jax
import jax.numpy as jnp
from jax import lax

F = 6
NLON = 2880
LEV = 32
LAT_DEV = 16
KMAX = 1024
KMIN = 32
NPOL = 2
CAP = 14
NLAT = 128
N_LAT = 8


def listing(key):
    tiles = jnp.concatenate([jnp.arange(NPOL, dtype=jnp.int32), N_LAT - NPOL + jnp.arange(NPOL, dtype=jnp.int32)])
    keys = jax.random.split(jax.random.fold_in(key, 11), 2 * NPOL)
    lifts = jax.random.randint(jax.random.fold_in(key, 13), (2 * NPOL,), 0, 2).astype(jnp.int32)
    lifts = lifts.at[0].set(1).at[2 * NPOL - 1].set(0)
    offsets = jnp.arange(LAT_DEV, dtype=jnp.int32)

    def one_block(single, lift):
        order = jax.random.permutation(single, LAT_DEV - 1).astype(jnp.int32)
        dropped = order[:LAT_DEV - CAP] + lift
        gone = jnp.sum((offsets[:, None] == dropped[None, :]).astype(jnp.int32), axis=1)
        ranking = jnp.where(gone > 0, LAT_DEV + offsets, offsets)
        return jnp.argsort(ranking, stable=True)[:CAP].astype(jnp.int32)
    picks = jax.vmap(one_block)(keys, lifts)
    return (tiles[:, None] * LAT_DEV + picks).reshape(-1).astype(jnp.int32)


def draw_polar_rows(key, part):
    return listing(key)


def draw_bands(key, part):
    rows = listing(key)
    half = NPOL * CAP
    north = rows[:half]
    south = NLAT - 1 - rows[half:]
    far_north = jnp.maximum(jnp.max(north), 1)
    far_south = jnp.maximum(jnp.max(south), 1)
    band_north = KMIN + (KMAX - KMIN) * north // far_north
    band_south = KMIN + (KMAX - KMIN) * south // far_south
    return jnp.concatenate([band_north, band_south]).astype(jnp.int32)


def draw_inv_cos(key, part):
    rows = jnp.arange(NLAT, dtype=jnp.float32)
    middle = (NLAT - 1) / 2.0
    spread_pos = jnp.abs(rows - middle) / middle
    base = 1.0 + 7.0 * spread_pos * spread_pos * spread_pos
    jitter = jax.random.uniform(jax.random.fold_in(key, 31), (NLAT,), jnp.float32, 0.95, 1.05)
    return (base * jitter).astype(jnp.float32)


def steps_of(own_key, extent, pieces, least, high):
    def one(axis_at, parts):
        steps = jax.random.uniform(jax.random.fold_in(jax.random.fold_in(own_key, 6), axis_at), (parts,), jnp.float32, least / len(pieces), high / len(pieces))
        return jnp.repeat(jnp.exp(steps), extent[axis_at] // parts).reshape((-1,) + (1,) * (len(extent) - axis_at - 1))

    factor_of = one(*pieces[0])
    for cut in pieces[1:]:
        factor_of = factor_of * one(*cut)
    return factor_of


def noise(rng, dims, scale, bound, cuts=(), held_as=jnp.bfloat16):
    loudness = steps_of(rng, dims, cuts, -0.22, 0.18) if cuts else 1.0
    values = jax.random.normal(rng, dims, jnp.float32) * scale * loudness
    return jnp.minimum(jnp.maximum(values, -bound), bound).astype(held_as)


def setup_inputs(seed: int = 0) -> dict:
    key_list = jax.random.split(jax.random.key(seed), 7)
    fields = noise(key_list[0], (F, LEV, NLAT, NLON), 1.0, 6.0, ((2, 8), (3, 4)), jnp.float32)
    inv_cos = draw_inv_cos(jax.random.fold_in(key_list[6], 71), 0)
    coupling_lon = noise(key_list[2], (F, F), 0.08, 0.4, (), jnp.float32)
    coupling_lat = noise(key_list[3], (F, F), 0.3, 1.5, (), jnp.float32)
    polar_rows = draw_polar_rows(jax.random.fold_in(key_list[6], 71), 0)
    bands = draw_bands(jax.random.fold_in(key_list[6], 71), 0)
    return dict(fields=fields, inv_cos=inv_cos, coupling_lon=coupling_lon, coupling_lat=coupling_lat, polar_rows=polar_rows, bands=bands)


def difference(padded, axis, count):
    def shifted(offset):
        return lax.slice_in_dim(padded, 3 + offset, 3 + offset + count, axis=axis)
    return (45.0 * (shifted(1) - shifted(-1)) - 9.0 * (shifted(2) - shifted(-2)) + (shifted(3) - shifted(-3))) / 60.0


def fourier_table(length, modes):
    cells = jnp.arange(length, dtype=jnp.int32)
    waves = jnp.arange(modes, dtype=jnp.int32)
    phase = ((cells[:, None] * waves[None, :]) % length).astype(jnp.float32) * (2.0 * math.pi / length)
    return jnp.concatenate([jnp.cos(phase), jnp.sin(phase)], axis=1)


def mode_weights(band_each, modes, length):
    columns = jnp.arange(2 * modes, dtype=jnp.int32) % modes
    keep = columns[None, :] < band_each[:, None]
    factor = jnp.where(columns == 0, 1.0, 2.0) / length
    return jnp.where(keep, factor[None, :], 0.0).astype(jnp.float32)


def advance(fields, padded_lat, padded_lon, inv_cos, coupling_lon, coupling_lat):
    along_lat = difference(padded_lat, 2, fields.shape[2])
    along_lon = difference(padded_lon, 3, fields.shape[3]) * inv_cos[None, None, :, None]
    change = jnp.einsum("fg,glrn->flrn", coupling_lon, along_lon, precision=lax.Precision.HIGHEST)
    change = change + jnp.einsum("fg,glrn->flrn", coupling_lat, along_lat, precision=lax.Precision.HIGHEST)
    return fields + change


def reference(fields, inv_cos, coupling_lon, coupling_lat, polar_rows, bands):
    padded_lat = jnp.pad(fields, ((0, 0), (0, 0), (3, 3), (0, 0)))
    padded_lon = jnp.concatenate([fields[..., -3:], fields, fields[..., :3]], axis=3)
    predicted = advance(fields, padded_lat, padded_lon, inv_cos, coupling_lon, coupling_lat)
    listed = predicted[:, :, polar_rows, :]
    table = fourier_table(NLON, KMAX)
    spectra = jnp.einsum("flin,nk->flik", listed, table, precision=lax.Precision.HIGHEST)
    weights = mode_weights(bands, KMAX, NLON)
    filtered = jnp.einsum("flik,nk->flin", spectra * weights[None, None], table, precision=lax.Precision.HIGHEST)
    return predicted.at[:, :, polar_rows, :].set(filtered)
```

```python
import functools
import math

import jax
import jax.numpy as jnp
import numpy as np
from jax import lax
from jax.experimental import pallas as pl
from jax.experimental.pallas import tpu as pltpu
from jax.sharding import PartitionSpec as P

KMAX = 1024
CAP = 14
SUB = 8
LANE = 128
HALO = 3
GROUPS_PER_CHUNK = 1


VMEM = pltpu.VMEM
SMEM = pltpu.SMEM


def whole(space):
    return pl.BlockSpec(memory_space=space)


def resident(shape):
    zeros = (0,) * len(shape)
    return pl.BlockSpec(shape, lambda *_: zeros)


def stencil_kernel(
    dims,
    place_ref,
    inv_cos_ref,
    lon_ref,
    lat_ref,
    polar_ref,
    fields_ref,
    north_ref,
    south_ref,
    edge_ref,
    out_ref,
    *rest,
):
    fc, rows, n, width, per, count = dims
    sends = rest[:count]
    q_ref, d_ref = rest[count:]
    off = n % LANE
    for f in range(fc):
        for r in range(HALO):
            q_ref[f, r] = north_ref[f, r]
            q_ref[f, rows + HALO + r] = south_ref[f, r]

    def load_field(f, carry):
        for lo in range(0, n, LANE):
            hi = min(lo + LANE, n)
            turned = jnp.swapaxes(fields_ref[f, :, :, lo:hi], 0, 1)
            q_ref[f, HALO : HALO + rows, :, lo:hi] = turned
        q_ref[f, HALO : HALO + rows, :, n:] = edge_ref[f, :, :, off:]
        return carry

    lax.fori_loop(0, fc, load_field, 0)

    def row(r, carry):
        scale = inv_cos_ref[r]
        for f in range(fc):
            q = q_ref[f, r + HALO]
            acc = 45.0 * (pltpu.roll(q, width - 1, 1) - pltpu.roll(q, 1, 1))
            acc = acc - 9.0 * (pltpu.roll(q, width - 2, 1) - pltpu.roll(q, 2, 1))
            acc = acc + (pltpu.roll(q, width - 3, 1) - pltpu.roll(q, 3, 1))
            d_ref[f] = acc * scale
        for tile in range(width // LANE):
            cut = slice(tile * LANE, (tile + 1) * LANE)
            dlon = [d_ref[g, :, cut] for g in range(fc)]
            dlat = []
            for g in range(fc):
                at = lambda o: q_ref[g, r + HALO + o, :, cut]
                dlat.append(
                    45.0 * (at(1) - at(-1)) - 9.0 * (at(2) - at(-2)) + (at(3) - at(-3))
                )
            for f in range(fc):
                acc = q_ref[f, r + HALO, :, cut]
                for g in range(fc):
                    acc = acc + lon_ref[f * fc + g] * dlon[g] + lat_ref[f * fc + g] * dlat[g]
                out_ref[f, r, :, cut] = acc
        return carry

    lax.fori_loop(0, rows, row, 0)

    me = place_ref[1]
    start = place_ref[2]
    base = place_ref[0] * rows

    @pl.when(place_ref[3] > 0)
    def _():
        for t in range(count):

            def pick(k, carry):
                p = jnp.minimum((me ^ t) * per + k, fc * CAP - 1)
                r = polar_ref[start + p // fc] - base
                sends[t][0, k] = out_ref[p % fc, r]
                return carry

            lax.fori_loop(0, per, pick, 0)


def stencil(place, inv_cos, lon, lat, polar, fields, north, south, edge, group0, groups, dims):
    fc, rows, n, width, per, count = dims
    levels = groups * SUB
    f32 = jnp.float32
    return pl.pallas_call(
        functools.partial(stencil_kernel, dims),
        grid=(groups,),
        in_specs=[whole(SMEM)] * 5
        + [
            pl.BlockSpec((fc, SUB, rows, n), lambda g: (0, group0 + g, 0, 0)),
            pl.BlockSpec((fc, HALO, SUB, width), lambda g: (0, 0, group0 + g, 0)),
            pl.BlockSpec((fc, HALO, SUB, width), lambda g: (0, 0, group0 + g, 0)),
            pl.BlockSpec((fc, rows, SUB, LANE), lambda g: (0, 0, group0 + g, 0)),
        ],
        out_specs=[pl.BlockSpec((fc, rows, SUB, width), lambda g: (0, 0, g, 0))]
        + [pl.BlockSpec((1, per, SUB, width), lambda g: (g, 0, 0, 0))] * count,
        out_shape=[jax.ShapeDtypeStruct((fc, rows, levels, width), f32)]
        + [jax.ShapeDtypeStruct((groups, per, SUB, width), f32)] * count,
        scratch_shapes=[
            VMEM((fc, rows + 2 * HALO, SUB, width), f32),
            VMEM((fc, SUB, width), f32),
        ],
        compiler_params=pltpu.CompilerParams(vmem_limit_bytes=40 << 20),
        cost_estimate=pl.CostEstimate(
            flops=100 * fc * rows * levels * width,
            bytes_accessed=12 * fc * rows * levels * width,
            transcendentals=0,
        ),
        name="stencil",
    )(place, inv_cos, lon, lat, polar, fields, north, south, edge)


def split(x):
    high = x.astype(jnp.bfloat16)
    return high, (x - high.astype(jnp.float32)).astype(jnp.bfloat16)


def product(left, high, low):
    a, b = left
    dot = functools.partial(jnp.dot, preferred_element_type=jnp.float32)
    return dot(a, high) + (dot(b, high) + dot(a, low))


def by_partner(pieces, me):
    count = len(pieces)
    bit = 1
    while bit < count:
        flag = (me & bit) > 0
        pieces = [jnp.where(flag, pieces[i ^ bit], pieces[i]) for i in range(count)]
        bit *= 2
    return pieces


def filter_kernel(dims, length, place_ref, bands_ref, th_ref, tl_ref, uh_ref, ul_ref, *rest):
    fc, rows, n, width, per, count = dims
    inputs, outputs = rest[:count], rest[count : 2 * count]
    left_ref, low_ref, spec_ref, band_ref, back_ref = rest[2 * count :]
    me = place_ref[1]
    start = place_ref[2]
    parts = count // 4
    m = per * SUB
    quarter = KMAX // 4

    @pl.when(place_ref[3] > 0)
    def _():
        def set_band(k, carry):
            p = jnp.minimum(me * per + k, fc * CAP - 1)
            band_ref[pl.ds(pl.multiple_of(k * SUB, SUB), SUB), :] = jnp.full(
                (SUB, quarter), bands_ref[start + p // fc], jnp.int32
            )
            return carry

        lax.fori_loop(0, per, set_band, 0)
        x = by_partner([ref[0].reshape(m, width) for ref in inputs], me)
        for s in range(parts):
            x0, x1, x2, x3 = (x[i * parts + s] for i in range(4))
            e0, e1 = x0 + x2, x1 + x3
            cut = slice(s * width, (s + 1) * width)
            for i, y in enumerate((e0 + e1, e0 - e1, x0 - x2, x1 - x3)):
                high, low = split(y)
                left_ref[i * m : (i + 1) * m, cut] = high
                low_ref[i * m : (i + 1) * m, cut] = low

        def forward(lo, hi, col):
            cols = slice(col, col + quarter)
            return product(
                (left_ref[lo * m : hi * m], low_ref[lo * m : hi * m]),
                th_ref[:, cols],
                tl_ref[:, cols],
            )

        waves = 4 * lax.broadcasted_iota(jnp.int32, (m, quarter), 1)

        def weight(residue):
            k = waves + residue
            factor = jnp.where(k == 0, 1.0 / length, 2.0 / length)
            return jnp.where(k < band_ref[...], factor, 0.0)

        def keep(lo, col, value):
            high, low = split(value)
            spec_ref[0, lo * m : (lo + 1) * m, col * quarter : (col + 1) * quarter] = high
            spec_ref[1, lo * m : (lo + 1) * m, col * quarter : (col + 1) * quarter] = low

        for i in range(2):
            w = weight(2 * i)
            for c in range(2):
                keep(i, c, forward(i, i + 1, (2 * i + c) * quarter) * w)
        for i in range(2):
            w = weight(2 * i + 1)
            sign = 1.0 if i == 0 else -1.0
            cosine = forward(2, 4, (4 + i) * quarter)
            sine = forward(2, 4, (6 + i) * quarter)
            c = (cosine[:m] - sign * sine[m:]) * w
            s = (sine[:m] + sign * cosine[m:]) * w
            keep(2, i, c)
            keep(2, 2 + i, s)
            keep(3, i, sign * s)
            keep(3, 2 + i, -sign * c)

        def inverse(lo, hi, terms, row, cut):
            return product(
                (
                    spec_ref[0, lo * m : hi * m, : terms * quarter],
                    spec_ref[1, lo * m : hi * m, : terms * quarter],
                ),
                uh_ref[row * quarter : (row + terms) * quarter, cut],
                ul_ref[row * quarter : (row + terms) * quarter, cut],
            )

        for s in range(parts):
            for c in range(width // LANE):
                cut = slice(s * width + c * LANE, s * width + (c + 1) * LANE)
                even = inverse(0, 1, 2, 0, cut)
                half = inverse(1, 2, 2, 2, cut)
                odd = inverse(2, 4, 4, 4, cut)
                o0, o1 = odd[:m], odd[m:]
                p, d = even + half, even - half
                lanes = slice(c * LANE, (c + 1) * LANE)
                for i, y in enumerate((p + o0, d + o1, p - o0, d - o1)):
                    back_ref[i * parts + s, :, lanes] = y
        y = by_partner([back_ref[j] for j in range(count)], me)
        for t in range(count):
            outputs[t][0] = y[t].reshape(per, SUB, width)


def polar_filter(place, bands, tables, pieces, dims, length):
    fc, rows, n, width, per, count = dims
    groups = pieces[0].shape[0]
    m = per * SUB
    parts = count // 4
    f32, bf16 = jnp.float32, jnp.bfloat16
    spec = pl.BlockSpec((1, per, SUB, width), lambda g: (g, 0, 0, 0))
    return pl.pallas_call(
        functools.partial(filter_kernel, dims, length),
        grid=(groups,),
        in_specs=[whole(SMEM)] * 2 + [resident(t.shape) for t in tables] + [spec] * count,
        out_specs=[spec] * count,
        out_shape=[jax.ShapeDtypeStruct((groups, per, SUB, width), f32)] * count,
        scratch_shapes=[
            VMEM((4 * m, parts * width), bf16),
            VMEM((4 * m, parts * width), bf16),
            VMEM((2, 4 * m, KMAX), bf16),
            VMEM((m, KMAX // 4), jnp.int32),
            VMEM((count, m, width), f32),
        ],
        compiler_params=pltpu.CompilerParams(vmem_limit_bytes=56 << 20),
        cost_estimate=pl.CostEstimate(
            flops=18 * groups * m * width * parts * 4 * KMAX,
            bytes_accessed=8 * groups * count * m * width,
            transcendentals=0,
        ),
        name="polar_filter",
    )(place, bands, *tables, *pieces)


def fourier_tables(length, n, width, parts):
    f32, bf16 = jnp.float32, jnp.bfloat16
    quarter = KMAX // 4
    q = 4 * np.arange(quarter)
    waves = [(q, 0), (q, 1), (q + 2, 0), (q + 2, 1), (q + 1, 0), (q + 3, 0), (q + 1, 1), (q + 3, 1)]
    wave = jnp.asarray(np.concatenate([w for w, _ in waves]).astype(np.int32))
    is_sine = jnp.asarray(np.concatenate([np.full(quarter, s) for _, s in waves]).astype(np.int32))
    step = 32

    def circle(number):
        phase = (number % length).astype(f32) * (2.0 * math.pi / length)
        return jnp.cos(phase), jnp.sin(phase)

    def high_low(x):
        high = lax.reduce_precision(x, exponent_bits=8, mantissa_bits=7)
        return high.astype(bf16), (x - high).astype(bf16)

    lane = jnp.arange(parts * width, dtype=jnp.int32) % width
    cell = jnp.arange(parts * width, dtype=jnp.int32) // width * n + lane
    big = jnp.arange(width // step, dtype=jnp.int32) * step
    blocks = []
    for s in range(parts):
        c1, s1 = circle((big[:, None] + s * n) * wave[None, :])
        c2, s2 = circle(jnp.arange(step, dtype=jnp.int32)[:, None] * wave[None, :])
        c1, s1, c2, s2 = lax.optimization_barrier((c1, s1, c2, s2))
        c1, s1, c2, s2 = c1[:, None], s1[:, None], c2[None], s2[None]
        both = jnp.where(is_sine > 0, s1 * c2 + c1 * s2, c1 * c2 - s1 * s2)
        inside = (big[:, None] + jnp.arange(step, dtype=jnp.int32)[None, :]) < n
        blocks.append(jnp.where(inside[:, :, None], both, 0.0).reshape(width, 2 * KMAX))
    table = blocks[0] if parts == 1 else jnp.concatenate(blocks, axis=0)
    lead = np.concatenate([w for w, _ in waves]).reshape(-1, step)
    first = jnp.asarray(lead[:, 0].astype(np.int32))
    c1, s1 = circle(first[:, None] * cell[None, :])
    c2, s2 = circle(jnp.asarray((lead[0] - lead[0, 0]).astype(np.int32))[:, None] * cell[None, :])
    c1, s1, c2, s2 = lax.optimization_barrier((c1, s1, c2, s2))
    c1, s1, c2, s2 = c1[:, None], s1[:, None], c2[None], s2[None]
    sine_row = jnp.repeat(jnp.asarray([s for _, s in waves], jnp.int32), quarter // step)
    both = jnp.where(sine_row[:, None, None] > 0, s1 * c2 + c1 * s2, c1 * c2 - s1 * s2)
    turned = jnp.where(lane < n, both, 0.0).reshape(2 * KMAX, parts * width)
    return high_low(table) + high_low(turned)


def merge_kernel(dims, aliased, place_ref, polar_ref, *rest):
    fc, rows, n, width, per, count = dims
    if aliased:
        rest = rest[1:]
    predicted_ref = rest[0]
    returned = rest[1 : 1 + count]
    out_ref, all_ref, slot_ref = rest[1 + count :]
    me = place_ref[1]
    start = place_ref[2]
    base = place_ref[0] * rows
    polar = place_ref[3] > 0
    for r in range(rows):
        slot_ref[r] = -1

    @pl.when(polar)
    def _():
        for c in range(CAP):
            slot_ref[polar_ref[start + c] - base] = c
        for t in range(count):
            all_ref[pl.ds((me ^ t) * per, per)] = returned[t][0]

    slots = [slot_ref[r] for r in range(rows)]

    def field(f, carry):
        for lo in range(0, n, LANE):
            hi = min(lo + LANE, n)
            picked = []
            for r, slot in enumerate(slots):
                smooth = all_ref[jnp.maximum(slot, 0) * fc + f, :, lo:hi]
                picked.append(jnp.where(slot >= 0, smooth, predicted_ref[f, r, :, lo:hi]))
            out_ref[f, :, :, lo:hi] = jnp.swapaxes(jnp.stack(picked), 0, 1)
        return carry

    lax.fori_loop(0, fc, field, 0)


def merge(place, polar, out, predicted, returned, group0, total, dims):
    fc, rows, n, width, per, count = dims
    groups = returned[0].shape[0]
    aliased = out is not None
    return pl.pallas_call(
        functools.partial(merge_kernel, dims, aliased),
        grid=(groups,),
        in_specs=[whole(SMEM)] * 2
        + [whole(pl.ANY)] * aliased
        + [pl.BlockSpec((fc, rows, SUB, width), lambda g: (0, 0, g, 0))]
        + [pl.BlockSpec((1, per, SUB, width), lambda g: (g, 0, 0, 0))] * count,
        out_specs=pl.BlockSpec((fc, SUB, rows, n), lambda g: (0, group0 + g, 0, 0)),
        out_shape=jax.ShapeDtypeStruct((fc, total, rows, n), jnp.float32),
        scratch_shapes=[
            VMEM((count * per, SUB, width), jnp.float32),
            SMEM((rows,), jnp.int32),
        ],
        input_output_aliases={2: 0} if aliased else {},
        compiler_params=pltpu.CompilerParams(vmem_limit_bytes=32 << 20),
        cost_estimate=pl.CostEstimate(
            flops=fc * rows * groups * SUB * width,
            bytes_accessed=12 * fc * rows * groups * SUB * width,
            transcendentals=0,
        ),
        name="merge",
    )(place, polar, *([out] if aliased else []), predicted, *returned)


def swap(pieces, ends, lat_count, count):
    axes = ("lat", "lon")
    tiles = list(range(ends)) + list(range(lat_count - ends, lat_count))
    relay = {a: a + ends if a < ends else a - ends for a in tiles}

    def at(a, o):
        return a * count + o

    out = [pieces[0]]
    for t in range(1, count):
        if count == 4 and t == 3 and lat_count >= 4 * ends:
            there = [(at(a, o), at(relay[a], o ^ t)) for a in tiles for o in range(count)]
            down = [(at(relay[a], o), at(a, o)) for a in tiles for o in range(count)]
            out.append(lax.ppermute(lax.ppermute(pieces[t], axes, there), axes, down))
        else:
            pairs = [(at(a, o), at(a, o ^ t)) for a in tiles for o in range(count)]
            out.append(lax.ppermute(pieces[t], axes, pairs))
    return out


def local(fields, inv_cos, coupling_lon, coupling_lat, polar_rows, bands):
    fc, levels, rows, n = fields.shape
    lat_count, count = lax.axis_size("lat"), lax.axis_size("lon")
    ends = polar_rows.shape[0] // (2 * CAP)
    width = -(-(n + 2 * HALO) // LANE) * LANE
    per = -(-fc * CAP // count)
    dims = (fc, rows, n, width, per, count)
    length = n * count
    parts = count // 4

    tile, me = lax.axis_index("lat"), lax.axis_index("lon")
    south_end = tile >= lat_count - ends
    is_polar = (tile < ends) | south_end
    order = jnp.where(south_end, tile - (lat_count - 2 * ends), tile)
    start = jnp.where(is_polar, order * CAP, 0)
    place = jnp.stack([tile, me, start, is_polar.astype(jnp.int32)]).astype(jnp.int32)

    def ring(x, axis, shift, closed):
        size = lax.axis_size(axis)
        pairs = [(i, (i + shift) % size) for i in range(size) if closed or 0 <= i + shift < size]
        return lax.ppermute(x, axis, pairs)

    pad = ((0, 0), (0, 0), (0, 0), (0, width - n))
    last_rows = jnp.pad(jnp.transpose(fields[:, :, rows - HALO :], (0, 2, 1, 3)), pad)
    first_rows = jnp.pad(jnp.transpose(fields[:, :, :HALO], (0, 2, 1, 3)), pad)
    last_cells = jnp.transpose(fields[..., n - HALO :], (0, 3, 2, 1))
    first_cells = jnp.transpose(fields[..., :HALO], (0, 3, 2, 1))
    before = ring(last_cells, "lon", 1, True)
    after = ring(first_cells, "lon", -1, True)
    north = ring(last_rows, "lat", 1, False)
    south = ring(first_rows, "lat", -1, False)
    off = n % LANE
    back = lambda x: jnp.transpose(x, (0, 2, 3, 1))
    edge = jnp.pad(back(after), ((0, 0), (0, 0), (0, 0), (off, LANE - off - HALO)))
    edge = edge + jnp.pad(back(before), ((0, 0), (0, 0), (0, 0), (LANE - HALO, 0)))

    tables = fourier_tables(length, n, width, parts)
    lon_flat = (coupling_lon / 60.0).reshape(-1)
    lat_flat = (coupling_lat / 60.0).reshape(-1)
    groups = levels // SUB
    step = min(GROUPS_PER_CHUNK, groups)
    chunks = []
    for group0 in range(0, groups, step):
        made = stencil(
            place, inv_cos, lon_flat, lat_flat, polar_rows,
            fields, north, south, edge, group0, step, dims,
        )
        chunks.append((group0, made[0], swap(made[1:], ends, lat_count, count)))
    later = []
    for group0, predicted, pieces in chunks:
        done = polar_filter(place, bands, tables, pieces, dims, length)
        later.append((group0, predicted, swap(done, ends, lat_count, count)))
    out = None
    for group0, predicted, returned in later:
        out = merge(place, polar_rows, out, predicted, returned, group0, levels, dims)
    return out


def solution(mesh):
    return jax.shard_map(
        local,
        mesh=mesh,
        in_specs=(P(None, None, "lat", "lon"), P("lat"), P(), P(), P(), P()),
        out_specs=P(None, None, "lat", "lon"),
        check_vma=False,
    )
```

```python
import functools
import math

import jax
import jax.numpy as jnp
from jax import lax
from jax.experimental import pallas as pl
from jax.experimental.pallas import tpu as pltpu
from jax.sharding import PartitionSpec as P


KMAX = 1024
CAP = 14
SUB = 8
LANE = 128
HALO = 3
THERE = ((0,), (1,), (2, 3))
BACK = ((0, 1), (2,), (3,))


VMEM = pltpu.VMEM
SMEM = pltpu.SMEM
F32 = jnp.float32
BF16 = jnp.bfloat16


def whole(space):
    return pl.BlockSpec(memory_space=space)


def shape(*dims, dtype=F32):
    return jax.ShapeDtypeStruct(dims, dtype)


def cost(flops, moved):
    return pl.CostEstimate(flops=int(flops), bytes_accessed=int(moved), transcendentals=0)


def limit(mib):
    return pltpu.CompilerParams(vmem_limit_bytes=mib << 20)


def turn_kernel(dims, cuts, fields_ref, all_ref, *rest):
    fc, levels, rows, n, width, _, _ = dims
    k = len(cuts)
    firsts, lasts = rest[:k], rest[k : 2 * k]
    head_ref, tail_ref, band_ref, buf_ref, sems = rest[2 * k :]
    groups = levels // SUB
    final = (n - 1) // LANE * LANE
    lane = lax.broadcasted_iota(jnp.int32, (SUB, LANE), 1)

    def copy(g, f):
        return pltpu.make_async_copy(
            fields_ref.at[f, pl.ds(g * SUB, SUB)], buf_ref.at[g % 2, f], sems.at[g % 2, f]
        )

    for f in range(fc):
        copy(0, f).start()
    offset = lax.broadcasted_iota(jnp.int32, band_ref.shape, 0) - LANE
    offset = offset - lax.broadcasted_iota(jnp.int32, band_ref.shape, 1)
    far = jnp.abs(offset)
    size = jnp.where(far == 1, 45.0, jnp.where(far == 2, -9.0, jnp.where(far == 3, 1.0, 0.0)))
    band_ref[...] = jnp.where(offset > 0, size, -size).astype(BF16)
    for g in range(groups):
        at = slice(g * SUB, (g + 1) * SUB)
        piece = [i for i, (lo, hi) in enumerate(cuts) if lo <= g * SUB < hi][0]
        inner = slice(g * SUB - cuts[piece][0], (g + 1) * SUB - cuts[piece][0])
        if g + 1 < groups:
            for f in range(fc):
                copy(g + 1, f).start()

        def field(f, carry):
            copy(g, f).wait()
            for lo in range(0, n, LANE):
                hi = min(lo + LANE, n)
                x = jnp.swapaxes(buf_ref[g % 2, f, :, :, lo:hi], 0, 1)
                all_ref[f, HALO : HALO + rows, at, lo:hi] = x
                for r in range(HALO):
                    firsts[piece][f, r, inner, lo:hi] = x[r]
                    lasts[piece][f, r, inner, lo:hi] = x[rows - HALO + r]
            pad = jnp.zeros((SUB, width - n), F32)
            for r in range(rows):
                all_ref[f, r + HALO, at, n:] = pad
            for r in range(HALO):
                firsts[piece][f, r, inner, n:] = pad
                lasts[piece][f, r, inner, n:] = pad
            for out_ref, lo, by in ((head_ref, 0, 0), (tail_ref, final, n - HALO - final)):
                packed = jnp.zeros((SUB, LANE), F32)
                for r in range(rows):
                    turned = pltpu.roll(all_ref[f, r + HALO, at, lo : lo + LANE], (HALO * r - by) % LANE, 1)
                    mine = (lane >= HALO * r) & (lane < HALO * (r + 1))
                    packed = jnp.where(mine, turned, packed)
                out_ref[f, at] = packed
            return carry

        lax.fori_loop(0, fc, field, 0)


def turn(fields, dims, cuts):
    fc, levels, rows, n, width, _, _ = dims
    row_shapes = [shape(fc, HALO, hi - lo, width) for lo, hi in cuts]
    shapes = [shape(fc, rows + 2 * HALO, levels, width)] + row_shapes * 2 + [shape(fc, levels, LANE)] * 2
    wide = 2 * LANE if width % (2 * LANE) == 0 else LANE
    shapes.append(shape(wide + 2 * LANE, wide, dtype=BF16))
    made = pl.pallas_call(
        functools.partial(turn_kernel, dims, cuts),
        in_specs=[whole(pltpu.HBM)],
        out_specs=[whole(VMEM)] * len(shapes),
        out_shape=shapes,
        scratch_shapes=[
            VMEM((2, fc, SUB, rows, n), F32),
            pltpu.SemaphoreType.DMA((2, fc)),
        ],
        compiler_params=limit(8),
        cost_estimate=cost(0, 8 * fc * levels * rows * width),
        name="turn",
    )(pltpu.with_memory_space_constraint(fields, pltpu.HBM))
    k = len(cuts)
    return made[0], made[1 : 1 + k], made[1 + k : 1 + 2 * k], *made[-3:]


def stencil_kernel(dims, plan, owned, ready, cuts_of, place_ref, inv_cos_ref, lon_ref, lat_ref, polar_ref, *rest):
    fc, _, rows, _, _, per, _ = dims
    k = len(cuts_of)
    norths, souths = rest[:k], rest[k : 2 * k]
    before_ref, after_ref, band_ref = rest[2 * k : 2 * k + 3]
    aliased = plan.aliased if plan else 0
    q_ref, new_ref, *sends = rest[2 * k + 4 + ready + aliased : -4]

    @pl.when((place_ref[3] > 0) == (plan is not None))
    def _():
        for own in owned:
            piece = [i for i, (lo, hi) in enumerate(cuts_of) if lo <= own * SUB < hi][0]
            here = slice(own * SUB, (own + 1) * SUB)
            there = slice(own * SUB - cuts_of[piece][0], (own + 1) * SUB - cuts_of[piece][0])
            for f in range(fc):
                for r in range(HALO):
                    q_ref[f, r, here] = norths[piece][f, r, there]
                    q_ref[f, rows + HALO + r, here] = souths[piece][f, r, there]

        def one(group, carry):
            predict(
                dims, group, inv_cos_ref, lon_ref, lat_ref, before_ref, after_ref, band_ref,
                q_ref, new_ref, *rest[-4:],
            )
            return carry

        lax.fori_loop(owned[0], owned[-1] + 1, one, 0)
        me = place_ref[1]
        unit = 3 if per % 3 == 0 and fc % 3 == 0 else 1
        for t, send in enumerate(sends):

            def pick(k, carry):
                p = jnp.minimum((me ^ t) * per + unit * k, fc * CAP - unit)
                c = lax.div(p, fc)
                r = polar_ref[place_ref[2] + c] - place_ref[0] * rows
                some = new_ref[owned[0], r, pl.ds(p - c * fc, unit)]
                send[plan.slot(t), pl.ds(unit * k, unit)] = some
                return carry

            lax.fori_loop(0, per // unit, pick, 0)


def predict(
    dims, group, inv_cos_ref, lon_ref, lat_ref, before_ref, after_ref, band_ref,
    q_ref, new_ref, factor_ref, high_ref, low_ref, dlon_ref,
):
    fc, _, rows, n, width, _, _ = dims
    off = n % LANE
    lane = lax.broadcasted_iota(jnp.int32, (SUB, LANE), 1)
    at = pl.ds(pl.multiple_of(group * SUB, SUB), SUB)
    tiles = width // LANE
    cuts = [slice(i * LANE, (i + 1) * LANE) for i in range(tiles)]
    for f in range(fc):
        for k in range(fc):
            factor_ref[0, f, k] = jnp.full((SUB, LANE), lon_ref[f, k] * (1.0 / 60.0), F32)
            factor_ref[1, f, k] = jnp.full((SUB, LANE), lat_ref[f, k] * (1.0 / 60.0), F32)

    def lay(r2, carry):
        for f in range(fc):
            base = pl.multiple_of((f * rows + 2 * r2) * SUB, 2 * SUB)
            after, before = after_ref[f, at], before_ref[f, at]
            for i in range(tiles):
                x = q_ref[f, pl.ds(HALO + 2 * r2, 2), at, cuts[i]]
                if i == tiles - 1:
                    edge = []
                    for k in range(2):
                        shift = HALO * (2 * r2 + k)
                        right = pltpu.roll(after, lax.rem(off + HALO * LANE - shift, LANE), 1)
                        left = pltpu.roll(before, LANE - HALO - shift, 1)
                        edge.append(jnp.where(lane < off + HALO, right, left))
                    x = jnp.where((lane < off)[None], x, jnp.stack(edge))
                high, low = split(x.reshape(2 * SUB, LANE))
                for spot in [i + 1] + [0] * (i == tiles - 1) + [tiles + 1] * (i == 0):
                    cut = slice(spot * LANE, (spot + 1) * LANE)
                    high_ref[pl.ds(base, 2 * SUB), cut] = high
                    low_ref[pl.ds(base, 2 * SUB), cut] = low
        return carry

    lax.fori_loop(0, rows // 2, lay, 0)
    wide = band_ref.shape[1]
    for lo in range(0, width, wide):
        window = slice(lo, lo + wide + 2 * LANE)
        dot = functools.partial(jnp.dot, preferred_element_type=F32)
        both = dot(high_ref[:, window], band_ref[...]) + dot(low_ref[:, window], band_ref[...])
        dlon_ref[:, lo : lo + wide] = both

    def row(r, carry):
        scale = inv_cos_ref[r]
        for cut in cuts:
            dlon, dlat = [], []
            for f in range(fc):
                spot = pl.multiple_of((f * rows + r) * SUB, SUB)
                dlon.append(dlon_ref[pl.ds(spot, SUB), cut] * scale)
                q = lambda o: q_ref[f, r + HALO + o, at, cut]
                dlat.append(45.0 * (q(1) - q(-1)) - 9.0 * (q(2) - q(-2)) + (q(3) - q(-3)))
            for f in range(fc):
                acc = q_ref[f, r + HALO, at, cut]
                for k in range(fc):
                    acc = acc + (factor_ref[0, f, k] * dlon[k] + factor_ref[1, f, k] * dlat[k])
                new_ref[group, r, f, :, cut] = acc
        return carry

    lax.fori_loop(0, rows, row, 0)


class Plan:
    def __init__(self, group, parts, count, relayed, earlier):
        part = [p for p in parts if group in p][0]
        self.size = len(part)
        self.inside = part.index(group)
        self.part = part
        self.direct = [t for t in range(1, count) if t not in relayed]
        self.earlier = [earlier[t] for t in self.direct] if self.inside else []
        self.aliased = len(self.earlier)

    def slot(self, t):
        return self.inside if t in self.direct else 0

    def shapes(self, dims):
        _, _, _, _, width, per, count = dims
        return [
            shape(self.size if t in self.direct else 1, per, SUB, width) for t in range(count)
        ]

    def aliases(self, first_in, first_out):
        return {first_in + i: first_out + t for i, t in enumerate(self.direct) if self.aliased}


def stencil(scalars, halos, cuts, before, after, band, turned, new, owned, plan, dims):
    fc, levels, rows, _, width, _, _ = dims
    groups = levels // SUB
    sends = plan.shapes(dims) if plan else []
    earlier = plan.earlier if plan else []
    arrays = [*halos, before, after, band, turned]
    first = len(scalars) + len(arrays)
    aliases = {first - 1: 0}
    ready = new is not None
    if ready:
        arrays.append(new)
        aliases[first] = 1
    if plan:
        aliases.update(plan.aliases(first + ready, 2))
    return pl.pallas_call(
        functools.partial(stencil_kernel, dims, plan, owned, ready, cuts),
        in_specs=[whole(SMEM)] * 5 + [whole(VMEM)] * (len(arrays) + len(earlier)),
        out_specs=[whole(VMEM)] * (2 + len(sends)),
        out_shape=[shape(*turned.shape), shape(groups, rows, fc, SUB, width)] + sends,
        scratch_shapes=[
            VMEM((2, fc, fc, SUB, LANE), F32),
            VMEM((fc * rows * SUB, width + 2 * LANE), BF16),
            VMEM((fc * rows * SUB, width + 2 * LANE), BF16),
            VMEM((fc * rows * SUB, width), F32),
        ],
        input_output_aliases=aliases,
        compiler_params=limit(12),
        cost_estimate=cost(100 * fc * rows * SUB * width, 12 * fc * rows * SUB * width),
        name="stencil",
    )(*scalars, *arrays, *earlier)


def table_kernel(dims, length, high_ref, low_ref, base_ref, step_ref):
    _, _, _, n, width, _, count = dims
    parts = count // 4
    quarter = KMAX // 4
    step = 32
    column = lax.broadcasted_iota(jnp.int32, (1, KMAX), 1)
    block = column // quarter
    residue = jnp.where(block == 1, 2, jnp.where(block == 2, 1, block))
    wave = 4 * (column - block * quarter) + residue

    def circle(cell):
        number = (cell * wave).astype(F32)
        turns = jnp.floor(number * (1.0 / length))
        phase = (number - turns * length) * (2.0 * math.pi / length)
        return jnp.cos(phase), jnp.sin(phase)

    c2, s2 = circle(lax.broadcasted_iota(jnp.int32, (step, KMAX), 0))
    step_ref[0], step_ref[1] = c2, s2
    blocks = width // step
    for s in range(parts):
        c1, s1 = circle(step * lax.broadcasted_iota(jnp.int32, (blocks, KMAX), 0) + s * n)
        base_ref[0], base_ref[1] = c1, s1

        def band(a, carry):
            c1, s1 = base_ref[0, pl.ds(a, 1), :], base_ref[1, pl.ds(a, 1), :]
            inside = a * step + lax.broadcasted_iota(jnp.int32, (step, quarter), 0) < n
            at = pl.ds(pl.multiple_of(s * width + a * step, step), step)
            for i in range(4):
                cut = slice(i * quarter, (i + 1) * quarter)
                c2, s2 = step_ref[0, :, cut], step_ref[1, :, cut]
                cosine = c1[:, cut] * c2 - s1[:, cut] * s2
                sine = s1[:, cut] * c2 + c1[:, cut] * s2
                for value, col in ((cosine, (0, 2, 4, 5)[i]), (sine, (1, 3, 6, 7)[i])):
                    value = jnp.where(inside, value, 0.0)
                    high, low = split(value)
                    out = slice(col * quarter, (col + 1) * quarter)
                    high_ref[at, out] = high
                    low_ref[at, out] = low
            return carry

        lax.fori_loop(0, blocks, band, 0)


def tables(dims, length):
    _, _, _, _, width, _, count = dims
    out = shape(count // 4 * width, 2 * KMAX, dtype=BF16)
    return pl.pallas_call(
        functools.partial(table_kernel, dims, length),
        out_specs=[whole(VMEM)] * 2,
        out_shape=[out] * 2,
        scratch_shapes=[VMEM((2, width // 32, KMAX), F32), VMEM((2, 32, KMAX), F32)],
        compiler_params=limit(4),
        cost_estimate=cost(20 * count // 4 * width * 2 * KMAX, 4 * count // 4 * width * 2 * KMAX),
        name="tables",
    )()


def split(x):
    high = x.astype(BF16)
    return high, (x - high.astype(F32)).astype(BF16)


def product(left, high, low, turned):
    half = left.shape[0] // 2
    dims = (((1,), (1 if turned else 0,)), ((), ()))
    dot = lambda x, y: lax.dot_general(x, y, dims, preferred_element_type=F32)
    both = dot(left, high)
    return both[:half] + (both[half:] + dot(left[:half], low))


def by_partner(pieces, me):
    count = len(pieces)
    bit = 1
    while bit < count:
        flag = (me & bit) > 0
        pieces = [jnp.where(flag, pieces[i ^ bit], pieces[i]) for i in range(count)]
        bit *= 2
    return pieces


def filter_kernel(dims, source, plan, length, place_ref, bands_ref, high_ref, low_ref, *rest):
    fc, _, _, _, width, per, count = dims
    inputs, outputs = rest[:count], rest[count + plan.aliased :][:count]
    left_ref, spec_ref, band_ref = rest[-3:]
    me = place_ref[1]
    parts = count // 4
    m = per * SUB
    quarter = KMAX // 4

    @pl.when(place_ref[3] > 0)
    def _():
        for p in range(count * per):
            c = min(p // fc, CAP - 1)
            band_ref[p * SUB : (p + 1) * SUB] = jnp.full(
                (SUB, LANE), bands_ref[place_ref[2] + c], jnp.int32
            )
        mine = pl.ds(pl.multiple_of(me * m, SUB), m)
        band = jnp.concatenate([band_ref[mine]] * (quarter // LANE), axis=1)
        waves = 4 * lax.broadcasted_iota(jnp.int32, (m, quarter), 1)

        def weight(residue):
            k = waves + residue
            factor = jnp.where(k == 0, 1.0 / length, 2.0 / length)
            return jnp.where(k < band, factor, 0.0)

        def spot(i, term):
            return (2 * i + term) * m if i < 2 else (4 + (i - 2) + 2 * term) * m

        def keep(i, col, value):
            for term, x in enumerate(split(value)):
                spec_ref[spot(i, term) : spot(i, term) + m, col * quarter : (col + 1) * quarter] = x

        for lo in range(0, width, LANE):
            lanes = slice(lo, lo + LANE)
            x = by_partner(
                [ref[source.slot(t), :, :, lanes].reshape(m, LANE) for t, ref in enumerate(inputs)], me
            )
            for s in range(parts):
                x0, x1, x2, x3 = (x[i * parts + s] for i in range(4))
                e0, e1 = x0 + x2, x1 + x3
                cut = slice(s * width + lo, s * width + lo + LANE)
                for i, y in enumerate((e0 + e1, e0 - e1, x0 - x2, x1 - x3)):
                    for term, z in enumerate(split(y)):
                        left_ref[spot(i, term) : spot(i, term) + m, cut] = z

        for i in range(2):
            w = weight(2 * i)
            for c in range(2):
                cols = slice((2 * i + c) * quarter, (2 * i + c + 1) * quarter)
                left = left_ref[2 * m * i : 2 * m * (i + 1)]
                keep(i, c, product(left, high_ref[:, cols], low_ref[:, cols], False) * w)

        def forward(col):
            cols = slice(col * quarter, (col + 1) * quarter)
            return product(left_ref[4 * m :], high_ref[:, cols], low_ref[:, cols], False)

        for i in range(2):
            w = weight(2 * i + 1)
            cosine, sine = forward(4 + i), forward(6 + i)
            if i == 0:
                c = (cosine[:m] - sine[m:]) * w
                s = (sine[:m] + cosine[m:]) * w
            else:
                c = (cosine[:m] + sine[m:]) * w
                s = (sine[:m] - cosine[m:]) * w
            keep(2, i, c)
            keep(2, 2 + i, s)
            keep(3, i, s if i == 0 else -s)
            keep(3, 2 + i, -c if i == 0 else c)

        wide = 2 * LANE if width % (2 * LANE) == 0 else LANE

        def inverse(rows_at, terms, col, cells):
            cols = slice(col * quarter, (col + terms) * quarter)
            left = spec_ref[rows_at, : terms * quarter]
            return product(left, high_ref[cells, cols], low_ref[cells, cols], True)

        def block(j, carry):
            lanes = pl.ds(pl.multiple_of(j * wide, wide), wide)
            pieces = [None] * count
            for s in range(parts):
                cells = pl.ds(pl.multiple_of(s * width + j * wide, wide), wide)
                whole_part = inverse(slice(0, 2 * m), 2, 0, cells)
                half = inverse(slice(2 * m, 4 * m), 2, 2, cells)
                odd = inverse(slice(4 * m, 8 * m), 4, 4, cells)
                o0, o1 = odd[:m], odd[m:]
                p, d = whole_part + half, whole_part - half
                for i, y in enumerate((p + o0, d + o1, p - o0, d - o1)):
                    pieces[i * parts + s] = y
            for t, y in enumerate(by_partner(pieces, me)):
                outputs[t][plan.slot(t), :, :, lanes] = y.reshape(per, SUB, wide)
            return carry

        lax.fori_loop(0, width // wide, block, 0)


def polar_filter(scalars, table, pieces, source, plan, dims, length):
    _, _, _, _, width, per, count = dims
    m = per * SUB
    parts = count // 4
    return pl.pallas_call(
        functools.partial(filter_kernel, dims, source, plan, length),
        in_specs=[whole(SMEM)] * 2 + [whole(VMEM)] * (2 + count + plan.aliased),
        out_specs=[whole(VMEM)] * count,
        out_shape=plan.shapes(dims),
        scratch_shapes=[
            VMEM((8 * m, parts * width), BF16),
            VMEM((8 * m, KMAX), BF16),
            VMEM((count * m, LANE), jnp.int32),
        ],
        input_output_aliases=plan.aliases(4 + count, 0),
        compiler_params=limit(12),
        cost_estimate=cost(18 * m * width * parts * 4 * KMAX, 8 * count * m * width),
        name="polar_filter",
    )(*scalars, *table, *pieces, *plan.earlier)


def merge_kernel(dims, plan, group, aliased, place_ref, polar_ref, *rest):
    fc, _, rows, n, _, per, count = dims
    if aliased:
        rest = rest[1:]
    predicted_ref = rest[0]
    returned = rest[1 : 1 + count]
    out_ref, turned_ref, all_ref, slot_ref, sems = rest[1 + count :]
    me = place_ref[1]
    for r in range(rows):
        slot_ref[r] = -1

    @pl.when(place_ref[3] > 0)
    def _():
        for c in range(CAP):
            slot_ref[polar_ref[place_ref[2] + c] - place_ref[0] * rows] = c
        for t in range(count):
            all_ref[pl.ds((me ^ t) * per, per)] = returned[t][plan.slot(t)]

    slots = [slot_ref[r] for r in range(rows)]

    def copy(f):
        return pltpu.make_async_copy(
            turned_ref.at[f], out_ref.at[f, pl.ds(group * SUB, SUB)], sems.at[f]
        )

    for f in range(fc):
        for lo in range(0, n, LANE):
            hi = min(lo + LANE, n)
            picked = []
            for r, slot in enumerate(slots):
                smooth = all_ref[jnp.maximum(slot, 0) * fc + f, :, lo:hi]
                picked.append(jnp.where(slot >= 0, smooth, predicted_ref[group, r, f, :, lo:hi]))
            turned_ref[f, :, :, lo:hi] = jnp.swapaxes(jnp.stack(picked), 0, 1)
        copy(f).start()
    for f in range(fc):
        copy(f).wait()


def merge(scalars, out, predicted, returned, group, plan, dims):
    fc, levels, rows, n, width, per, count = dims
    aliased = out is not None
    return pl.pallas_call(
        functools.partial(merge_kernel, dims, plan, group, aliased),
        in_specs=[whole(SMEM)] * 2 + [whole(pl.ANY)] * aliased + [whole(VMEM)] * (1 + count),
        out_specs=whole(pl.ANY),
        out_shape=shape(fc, levels, rows, n),
        scratch_shapes=[
            VMEM((fc, SUB, rows, n), F32),
            VMEM((count * per, SUB, width), F32),
            SMEM((rows,), jnp.int32),
            pltpu.SemaphoreType.DMA((fc,)),
        ],
        input_output_aliases={2: 0} if aliased else {},
        compiler_params=limit(8),
        cost_estimate=cost(fc * rows * SUB * width, 12 * fc * rows * SUB * width),
        name="merge",
    )(*scalars, *([out] if aliased else []), predicted, *returned)


def partner(piece, t, ends, lat_count, count):
    tiles = list(range(ends)) + list(range(lat_count - ends, lat_count))
    pairs = [(a * count + o, a * count + (o ^ t)) for a in tiles for o in range(count)]
    return lax.ppermute(piece, ("lat", "lon"), pairs)


def across(piece, t, ends, lat_count, count):
    near = [(a, a + ends) for a in range(ends)]
    near += [(lat_count - 1 - a, lat_count - 1 - a - ends) for a in range(ends)]
    pairs = [(a * count + o, b * count + (o ^ t)) for a, b in near for o in range(count)]
    return lax.ppermute(piece, ("lat", "lon"), pairs)


def home(piece, ends, lat_count, count):
    near = [(a, a + ends) for a in range(ends)]
    near += [(lat_count - 1 - a, lat_count - 1 - a - ends) for a in range(ends)]
    pairs = [(b * count + o, a * count + o) for a, b in near for o in range(count)]
    return lax.ppermute(piece, ("lat", "lon"), pairs)


def substep(fields, inv_cos, coupling_lon, coupling_lat, polar_rows, bands):
    fc, levels, rows, n = fields.shape
    lat_count, count = lax.axis_size("lat"), lax.axis_size("lon")
    ends = polar_rows.shape[0] // (2 * CAP)
    width = -(-(n + 2 * HALO) // LANE) * LANE
    per = -(-fc * CAP // count)
    dims = (fc, levels, rows, n, width, per, count)
    length = n * count

    tile, me = lax.axis_index("lat"), lax.axis_index("lon")
    south_end = tile >= lat_count - ends
    is_polar = (tile < ends) | south_end
    order = jnp.where(south_end, tile - (lat_count - 2 * ends), tile)
    start = jnp.where(is_polar, order * CAP, 0)
    place = jnp.stack([tile, me, start, is_polar.astype(jnp.int32)]).astype(jnp.int32)

    def ring(x, axis, shift, closed):
        size = lax.axis_size(axis)
        pairs = [(i, (i + shift) % size) for i in range(size) if closed or 0 <= i + shift < size]
        return lax.ppermute(x, axis, pairs)

    groups = levels // SUB
    place_of = (ends, lat_count, count)
    relayed = [3] if count == 4 and lat_count >= 4 * ends else []
    cuts = [(0, SUB), (SUB, levels)] if levels > SUB else [(0, levels)]
    fields, place = lax.optimization_barrier((fields, place))
    turned, firsts, lasts, head, tail, band = turn(fields, dims, cuts)
    north, south = [], []
    for i in range(len(cuts)):
        north.append(ring(lasts[i], "lat", 1, False))
        south.append(ring(firsts[i], "lat", -1, False))
    before = ring(tail, "lon", 1, True)
    after = ring(head, "lon", -1, True)
    table = tables(dims, length)

    def exchange(parts, make):
        plans, kept, arrived, earlier = [], [], [], None
        for group in range(groups):
            plan = Plan(group, parts, count, relayed, earlier)
            extra, pieces = make(group, plan)
            earlier = pieces
            got = list(pieces)
            for t in relayed:
                middle = across(pieces[t], t, *place_of)
                got[t] = home(middle, *place_of)
            plans.append(plan)
            kept.append(extra)
            arrived.append(got)
            if group == plan.part[-1]:
                for t in plan.direct:
                    moved = partner(pieces[t], t, *place_of)
                    for member in plan.part:
                        arrived[member][t] = moved
        return plans, kept, arrived

    alone = tuple((g,) for g in range(groups))
    there, back = (THERE, BACK) if groups == 4 else (alone, alone)
    new = None

    def advance(owned, plan):
        nonlocal turned, new
        known = [i for i, (lo, hi) in enumerate(cuts) if lo <= owned[-1] * SUB]
        halos = (*(north[i] for i in known), *(south[i] for i in known))
        turned, new, *sends = stencil(
            (place, inv_cos, coupling_lon, coupling_lat, polar_rows),
            halos, cuts[: len(known)], before, after, band, turned, new, owned, plan, dims,
        )
        return None, sends

    def beside_poles(group, plan):
        made = advance([group], plan)
        if group % 2 == 1 or group == groups - 1:
            advance(list(range(group - group % 2, group + 1)), None)
        return made

    sources, _, pieces = exchange(there, beside_poles)

    def smooth(group, plan):
        return None, polar_filter(
            (place, bands), table, pieces[group], sources[group], plan, dims, length
        )

    plans, _, returned = exchange(back, smooth)
    out = None
    for group in range(groups):
        out = merge(
            (place, polar_rows), out, new, returned[group], group, plans[group], dims
        )
    return out


def solution(mesh):
    return jax.shard_map(
        substep,
        mesh=mesh,
        in_specs=(P(None, None, "lat", "lon"), P("lat"), P(), P(), P(), P()),
        out_specs=P(None, None, "lat", "lon"),
        check_vma=False,
    )
```

```python
import functools
import math

import jax
import jax.numpy as jnp
from jax import lax
from jax.experimental import pallas as pl
from jax.experimental.pallas import tpu as pltpu
from jax.sharding import PartitionSpec as P


KMAX = 1024
CAP = 14
SUB = 8
LANE = 128
HALO = 3
THERE = ((0, 1), (2, 3))
BACK = ((0, 1), (2,), (3,))


VMEM = pltpu.VMEM
SMEM = pltpu.SMEM
F32 = jnp.float32
BF16 = jnp.bfloat16


def whole(space):
    return pl.BlockSpec(memory_space=space)


def shape(*dims, dtype=F32):
    return jax.ShapeDtypeStruct(dims, dtype)


def cost(flops, moved):
    return pl.CostEstimate(flops=int(flops), bytes_accessed=int(moved), transcendentals=0)


def limit(mib):
    return pltpu.CompilerParams(vmem_limit_bytes=mib << 20)


def turn_kernel(dims, cuts, fields_ref, all_ref, *rest):
    fc, levels, rows, n, width, _, _ = dims
    k = len(cuts)
    firsts, lasts = rest[:k], rest[k : 2 * k]
    head_ref, tail_ref, band_ref, buf_ref, sems = rest[2 * k :]
    groups = levels // SUB
    final = (n - 1) // LANE * LANE
    lane = lax.broadcasted_iota(jnp.int32, (SUB, LANE), 1)

    def copy(g, f):
        return pltpu.make_async_copy(
            fields_ref.at[f, pl.ds(g * SUB, SUB)], buf_ref.at[g % 2, f], sems.at[g % 2, f]
        )

    for f in range(fc):
        copy(0, f).start()
    offset = lax.broadcasted_iota(jnp.int32, band_ref.shape, 0) - LANE
    offset = offset - lax.broadcasted_iota(jnp.int32, band_ref.shape, 1)
    far = jnp.abs(offset)
    size = jnp.where(far == 1, 45.0, jnp.where(far == 2, -9.0, jnp.where(far == 3, 1.0, 0.0)))
    band_ref[...] = jnp.where(offset > 0, size, -size).astype(BF16)
    for g in range(groups):
        at = slice(g * SUB, (g + 1) * SUB)
        piece = [i for i, (lo, hi) in enumerate(cuts) if lo <= g * SUB < hi][0]
        inner = slice(g * SUB - cuts[piece][0], (g + 1) * SUB - cuts[piece][0])
        if g + 1 < groups:
            for f in range(fc):
                copy(g + 1, f).start()

        def field(f, carry):
            copy(g, f).wait()
            for lo in range(0, n, LANE):
                hi = min(lo + LANE, n)
                x = jnp.swapaxes(buf_ref[g % 2, f, :, :, lo:hi], 0, 1)
                all_ref[f, HALO : HALO + rows, at, lo:hi] = x
                for r in range(HALO):
                    firsts[piece][f, r, inner, lo:hi] = x[r]
                    lasts[piece][f, r, inner, lo:hi] = x[rows - HALO + r]
            pad = jnp.zeros((SUB, width - n), F32)
            for r in range(rows):
                all_ref[f, r + HALO, at, n:] = pad
            for r in range(HALO):
                firsts[piece][f, r, inner, n:] = pad
                lasts[piece][f, r, inner, n:] = pad
            for out_ref, lo, by in ((head_ref, 0, 0), (tail_ref, final, n - HALO - final)):
                packed = jnp.zeros((SUB, LANE), F32)
                for r in range(rows):
                    turned = pltpu.roll(all_ref[f, r + HALO, at, lo : lo + LANE], (HALO * r - by) % LANE, 1)
                    mine = (lane >= HALO * r) & (lane < HALO * (r + 1))
                    packed = jnp.where(mine, turned, packed)
                out_ref[f, at] = packed
            return carry

        lax.fori_loop(0, fc, field, 0)


def turn(fields, dims, cuts):
    fc, levels, rows, n, width, _, _ = dims
    row_shapes = [shape(fc, HALO, hi - lo, width) for lo, hi in cuts]
    shapes = [shape(fc, rows + 2 * HALO, levels, width)] + row_shapes * 2 + [shape(fc, levels, LANE)] * 2
    wide = 2 * LANE if width % (2 * LANE) == 0 else LANE
    shapes.append(shape(wide + 2 * LANE, wide, dtype=BF16))
    made = pl.pallas_call(
        functools.partial(turn_kernel, dims, cuts),
        in_specs=[whole(pltpu.HBM)],
        out_specs=[whole(VMEM)] * len(shapes),
        out_shape=shapes,
        scratch_shapes=[
            VMEM((2, fc, SUB, rows, n), F32),
            pltpu.SemaphoreType.DMA((2, fc)),
        ],
        compiler_params=limit(8),
        cost_estimate=cost(0, 8 * fc * levels * rows * width),
        name="turn",
    )(pltpu.with_memory_space_constraint(fields, pltpu.HBM))
    k = len(cuts)
    return made[0], made[1 : 1 + k], made[1 + k : 1 + 2 * k], *made[-3:]


def stencil_kernel(dims, plan, owned, ready, cuts_of, place_ref, inv_cos_ref, lon_ref, lat_ref, polar_ref, *rest):
    fc, _, rows, _, _, per, _ = dims
    k = len(cuts_of)
    norths, souths = rest[:k], rest[k : 2 * k]
    before_ref, after_ref, band_ref = rest[2 * k : 2 * k + 3]
    aliased = plan.aliased if plan else 0
    q_ref, new_ref, *sends = rest[2 * k + 4 + ready + aliased : -4]

    @pl.when((place_ref[3] > 0) == (plan is not None))
    def _():
        for own in owned:
            piece = [i for i, (lo, hi) in enumerate(cuts_of) if lo <= own * SUB < hi][0]
            here = slice(own * SUB, (own + 1) * SUB)
            there = slice(own * SUB - cuts_of[piece][0], (own + 1) * SUB - cuts_of[piece][0])
            for f in range(fc):
                for r in range(HALO):
                    q_ref[f, r, here] = norths[piece][f, r, there]
                    q_ref[f, rows + HALO + r, here] = souths[piece][f, r, there]

        def one(group, carry):
            predict(
                dims, group, inv_cos_ref, lon_ref, lat_ref, before_ref, after_ref, band_ref,
                q_ref, new_ref, *rest[-4:],
            )
            return carry

        lax.fori_loop(owned[0], owned[-1] + 1, one, 0)
        me = place_ref[1]
        unit = 3 if per % 3 == 0 and fc % 3 == 0 else 1
        for t, send in enumerate(sends):

            def pick(k, carry):
                p = jnp.minimum((me ^ t) * per + unit * k, fc * CAP - unit)
                c = lax.div(p, fc)
                r = polar_ref[place_ref[2] + c] - place_ref[0] * rows
                some = new_ref[owned[0], r, pl.ds(p - c * fc, unit)]
                send[plan.slot(t), pl.ds(unit * k, unit)] = some
                return carry

            lax.fori_loop(0, per // unit, pick, 0)


def predict(
    dims, group, inv_cos_ref, lon_ref, lat_ref, before_ref, after_ref, band_ref,
    q_ref, new_ref, factor_ref, high_ref, low_ref, dlon_ref,
):
    fc, _, rows, n, width, _, _ = dims
    off = n % LANE
    lane = lax.broadcasted_iota(jnp.int32, (SUB, LANE), 1)
    at = pl.ds(pl.multiple_of(group * SUB, SUB), SUB)
    tiles = width // LANE
    cuts = [slice(i * LANE, (i + 1) * LANE) for i in range(tiles)]
    for f in range(fc):
        for k in range(fc):
            factor_ref[0, f, k] = jnp.full((SUB, LANE), lon_ref[f, k] * (1.0 / 60.0), F32)
            factor_ref[1, f, k] = jnp.full((SUB, LANE), lat_ref[f, k] * (1.0 / 60.0), F32)

    def lay(r2, carry):
        for f in range(fc):
            base = pl.multiple_of((f * rows + 2 * r2) * SUB, 2 * SUB)
            after, before = after_ref[f, at], before_ref[f, at]
            for i in range(tiles):
                x = q_ref[f, pl.ds(HALO + 2 * r2, 2), at, cuts[i]]
                if i == tiles - 1:
                    edge = []
                    for k in range(2):
                        shift = HALO * (2 * r2 + k)
                        right = pltpu.roll(after, lax.rem(off + HALO * LANE - shift, LANE), 1)
                        left = pltpu.roll(before, LANE - HALO - shift, 1)
                        edge.append(jnp.where(lane < off + HALO, right, left))
                    x = jnp.where((lane < off)[None], x, jnp.stack(edge))
                high, low = split(x.reshape(2 * SUB, LANE))
                for spot in [i + 1] + [0] * (i == tiles - 1) + [tiles + 1] * (i == 0):
                    cut = slice(spot * LANE, (spot + 1) * LANE)
                    high_ref[pl.ds(base, 2 * SUB), cut] = high
                    low_ref[pl.ds(base, 2 * SUB), cut] = low
        return carry

    lax.fori_loop(0, rows // 2, lay, 0)
    wide = band_ref.shape[1]
    for lo in range(0, width, wide):
        window = slice(lo, lo + wide + 2 * LANE)
        dot = functools.partial(jnp.dot, preferred_element_type=F32)
        both = dot(high_ref[:, window], band_ref[...]) + dot(low_ref[:, window], band_ref[...])
        dlon_ref[:, lo : lo + wide] = both

    def row(r, carry):
        scale = inv_cos_ref[r]
        for cut in cuts:
            dlon, dlat = [], []
            for f in range(fc):
                spot = pl.multiple_of((f * rows + r) * SUB, SUB)
                dlon.append(dlon_ref[pl.ds(spot, SUB), cut] * scale)
                q = lambda o: q_ref[f, r + HALO + o, at, cut]
                dlat.append(45.0 * (q(1) - q(-1)) - 9.0 * (q(2) - q(-2)) + (q(3) - q(-3)))
            for f in range(fc):
                acc = q_ref[f, r + HALO, at, cut]
                for k in range(fc):
                    acc = acc + (factor_ref[0, f, k] * dlon[k] + factor_ref[1, f, k] * dlat[k])
                new_ref[group, r, f, :, cut] = acc
        return carry

    lax.fori_loop(0, rows, row, 0)


class Plan:
    def __init__(self, group, parts, count, relayed, earlier, halved=False):
        self.halved = relayed if halved else []
        part = [p for p in parts if group in p][0]
        self.size = len(part)
        self.inside = part.index(group)
        self.part = part
        self.direct = [t for t in range(1, count) if t not in relayed]
        self.earlier = [earlier[t] for t in self.direct] if self.inside else []
        self.aliased = len(self.earlier)

    def slot(self, t):
        return self.inside if t in self.direct else 0

    def pieces(self, per, count):
        found = []
        for t in range(count):
            stops = (per // 2, per) if t in self.halved else (per,)
            found += [(t, lo, hi) for lo, hi in zip((0, *stops), stops)]
        return found

    def shapes(self, dims):
        _, _, _, _, width, per, count = dims
        return [
            shape(self.size if t in self.direct else 1, hi - lo, SUB, width)
            for t, lo, hi in self.pieces(per, count)
        ]

    def aliases(self, first_in, first_out, per, count):
        if not self.aliased:
            return {}
        at = [t for t, _, _ in self.pieces(per, count)]
        return {first_in + i: first_out + at.index(t) for i, t in enumerate(self.direct)}


def stencil(scalars, halos, cuts, before, after, band, turned, new, owned, plan, dims):
    fc, levels, rows, _, width, per, count = dims
    groups = levels // SUB
    sends = plan.shapes(dims) if plan else []
    earlier = plan.earlier if plan else []
    arrays = [*halos, before, after, band, turned]
    first = len(scalars) + len(arrays)
    aliases = {first - 1: 0}
    ready = new is not None
    if ready:
        arrays.append(new)
        aliases[first] = 1
    if plan:
        aliases.update(plan.aliases(first + ready, 2, per, count))
    return pl.pallas_call(
        functools.partial(stencil_kernel, dims, plan, owned, ready, cuts),
        in_specs=[whole(SMEM)] * 5 + [whole(VMEM)] * (len(arrays) + len(earlier)),
        out_specs=[whole(VMEM)] * (2 + len(sends)),
        out_shape=[shape(*turned.shape), shape(groups, rows, fc, SUB, width)] + sends,
        scratch_shapes=[
            VMEM((2, fc, fc, SUB, LANE), F32),
            VMEM((fc * rows * SUB, width + 2 * LANE), BF16),
            VMEM((fc * rows * SUB, width + 2 * LANE), BF16),
            VMEM((fc * rows * SUB, width), F32),
        ],
        input_output_aliases=aliases,
        compiler_params=limit(12),
        cost_estimate=cost(100 * fc * rows * SUB * width, 12 * fc * rows * SUB * width),
        name="stencil",
    )(*scalars, *arrays, *earlier)


def table_kernel(dims, length, high_ref, low_ref, base_ref, step_ref):
    _, _, _, n, width, _, count = dims
    parts = count // 4
    quarter = KMAX // 4
    step = 32
    column = lax.broadcasted_iota(jnp.int32, (1, KMAX), 1)
    block = column // quarter
    residue = jnp.where(block == 1, 2, jnp.where(block == 2, 1, block))
    wave = 4 * (column - block * quarter) + residue

    def circle(cell):
        number = (cell * wave).astype(F32)
        turns = jnp.floor(number * (1.0 / length))
        phase = (number - turns * length) * (2.0 * math.pi / length)
        return jnp.cos(phase), jnp.sin(phase)

    c2, s2 = circle(lax.broadcasted_iota(jnp.int32, (step, KMAX), 0))
    step_ref[0], step_ref[1] = c2, s2
    blocks = width // step
    for s in range(parts):
        c1, s1 = circle(step * lax.broadcasted_iota(jnp.int32, (blocks, KMAX), 0) + s * n)
        base_ref[0], base_ref[1] = c1, s1

        def band(a, carry):
            c1, s1 = base_ref[0, pl.ds(a, 1), :], base_ref[1, pl.ds(a, 1), :]
            inside = a * step + lax.broadcasted_iota(jnp.int32, (step, quarter), 0) < n
            at = pl.ds(pl.multiple_of(s * width + a * step, step), step)
            for i in range(4):
                cut = slice(i * quarter, (i + 1) * quarter)
                c2, s2 = step_ref[0, :, cut], step_ref[1, :, cut]
                cosine = c1[:, cut] * c2 - s1[:, cut] * s2
                sine = s1[:, cut] * c2 + c1[:, cut] * s2
                for value, col in ((cosine, (0, 2, 4, 5)[i]), (sine, (1, 3, 6, 7)[i])):
                    value = jnp.where(inside, value, 0.0)
                    high, low = split(value)
                    out = slice(col * quarter, (col + 1) * quarter)
                    high_ref[at, out] = high
                    low_ref[at, out] = low
            return carry

        lax.fori_loop(0, blocks, band, 0)


def tables(dims, length):
    _, _, _, _, width, _, count = dims
    out = shape(count // 4 * width, 2 * KMAX, dtype=BF16)
    return pl.pallas_call(
        functools.partial(table_kernel, dims, length),
        out_specs=[whole(VMEM)] * 2,
        out_shape=[out] * 2,
        scratch_shapes=[VMEM((2, width // 32, KMAX), F32), VMEM((2, 32, KMAX), F32)],
        compiler_params=limit(4),
        cost_estimate=cost(20 * count // 4 * width * 2 * KMAX, 4 * count // 4 * width * 2 * KMAX),
        name="tables",
    )()


def split(x):
    high = x.astype(BF16)
    return high, (x - high.astype(F32)).astype(BF16)


def product(left, high, low, turned):
    half = left.shape[0] // 2
    dims = (((1,), (1 if turned else 0,)), ((), ()))
    dot = lambda x, y: lax.dot_general(x, y, dims, preferred_element_type=F32)
    both = dot(left, high)
    return both[:half] + (both[half:] + dot(left[:half], low))


def by_partner(pieces, me):
    count = len(pieces)
    bit = 1
    while bit < count:
        flag = (me & bit) > 0
        pieces = [jnp.where(flag, pieces[i ^ bit], pieces[i]) for i in range(count)]
        bit *= 2
    return pieces


def filter_kernel(dims, source, plan, length, place_ref, bands_ref, high_ref, low_ref, *rest):
    fc, _, _, _, width, per, count = dims
    inputs, outputs = rest[:count], rest[count + plan.aliased : -3]
    left_ref, spec_ref, band_ref = rest[-3:]
    me = place_ref[1]
    parts = count // 4
    m = per * SUB
    quarter = KMAX // 4

    @pl.when(place_ref[3] > 0)
    def _():
        for p in range(count * per):
            c = min(p // fc, CAP - 1)
            band_ref[p * SUB : (p + 1) * SUB] = jnp.full(
                (SUB, LANE), bands_ref[place_ref[2] + c], jnp.int32
            )
        mine = pl.ds(pl.multiple_of(me * m, SUB), m)
        band = jnp.concatenate([band_ref[mine]] * (quarter // LANE), axis=1)
        waves = 4 * lax.broadcasted_iota(jnp.int32, (m, quarter), 1)

        def weight(residue):
            k = waves + residue
            factor = jnp.where(k == 0, 1.0 / length, 2.0 / length)
            return jnp.where(k < band, factor, 0.0)

        def spot(i, term):
            return (2 * i + term) * m if i < 2 else (4 + (i - 2) + 2 * term) * m

        def keep(i, col, value):
            for term, x in enumerate(split(value)):
                spec_ref[spot(i, term) : spot(i, term) + m, col * quarter : (col + 1) * quarter] = x

        for lo in range(0, width, LANE):
            lanes = slice(lo, lo + LANE)
            x = by_partner(
                [ref[source.slot(t), :, :, lanes].reshape(m, LANE) for t, ref in enumerate(inputs)], me
            )
            for s in range(parts):
                x0, x1, x2, x3 = (x[i * parts + s] for i in range(4))
                e0, e1 = x0 + x2, x1 + x3
                cut = slice(s * width + lo, s * width + lo + LANE)
                for i, y in enumerate((e0 + e1, e0 - e1, x0 - x2, x1 - x3)):
                    for term, z in enumerate(split(y)):
                        left_ref[spot(i, term) : spot(i, term) + m, cut] = z

        for i in range(2):
            w = weight(2 * i)
            for c in range(2):
                cols = slice((2 * i + c) * quarter, (2 * i + c + 1) * quarter)
                left = left_ref[2 * m * i : 2 * m * (i + 1)]
                keep(i, c, product(left, high_ref[:, cols], low_ref[:, cols], False) * w)

        def forward(col):
            cols = slice(col * quarter, (col + 1) * quarter)
            return product(left_ref[4 * m :], high_ref[:, cols], low_ref[:, cols], False)

        for i in range(2):
            w = weight(2 * i + 1)
            cosine, sine = forward(4 + i), forward(6 + i)
            if i == 0:
                c = (cosine[:m] - sine[m:]) * w
                s = (sine[:m] + cosine[m:]) * w
            else:
                c = (cosine[:m] + sine[m:]) * w
                s = (sine[:m] - cosine[m:]) * w
            keep(2, i, c)
            keep(2, 2 + i, s)
            keep(3, i, s if i == 0 else -s)
            keep(3, 2 + i, -c if i == 0 else c)

        wide = 2 * LANE if width % (2 * LANE) == 0 else LANE

        def inverse(rows_at, terms, col, cells):
            cols = slice(col * quarter, (col + terms) * quarter)
            left = spec_ref[rows_at, : terms * quarter]
            return product(left, high_ref[cells, cols], low_ref[cells, cols], True)

        def block(j, carry):
            lanes = pl.ds(pl.multiple_of(j * wide, wide), wide)
            pieces = [None] * count
            for s in range(parts):
                cells = pl.ds(pl.multiple_of(s * width + j * wide, wide), wide)
                whole_part = inverse(slice(0, 2 * m), 2, 0, cells)
                half = inverse(slice(2 * m, 4 * m), 2, 2, cells)
                odd = inverse(slice(4 * m, 8 * m), 4, 4, cells)
                o0, o1 = odd[:m], odd[m:]
                p, d = whole_part + half, whole_part - half
                for i, y in enumerate((p + o0, d + o1, p - o0, d - o1)):
                    pieces[i * parts + s] = y
            found = by_partner(pieces, me)
            for (t, lo, hi), out_ref in zip(plan.pieces(per, count), outputs):
                y = found[t][lo * SUB : hi * SUB].reshape(hi - lo, SUB, wide)
                out_ref[plan.slot(t), :, :, lanes] = y
            return carry

        lax.fori_loop(0, width // wide, block, 0)


def polar_filter(scalars, table, pieces, source, plan, dims, length):
    _, _, _, _, width, per, count = dims
    m = per * SUB
    parts = count // 4
    return pl.pallas_call(
        functools.partial(filter_kernel, dims, source, plan, length),
        in_specs=[whole(SMEM)] * 2 + [whole(VMEM)] * (2 + count + plan.aliased),
        out_specs=[whole(VMEM)] * len(plan.shapes(dims)),
        out_shape=plan.shapes(dims),
        scratch_shapes=[
            VMEM((8 * m, parts * width), BF16),
            VMEM((8 * m, KMAX), BF16),
            VMEM((count * m, LANE), jnp.int32),
        ],
        input_output_aliases=plan.aliases(4 + count, 0, per, count),
        compiler_params=limit(12),
        cost_estimate=cost(18 * m * width * parts * 4 * KMAX, 8 * count * m * width),
        name="polar_filter",
    )(*scalars, *table, *pieces, *plan.earlier)


def merge_kernel(dims, plan, group, aliased, place_ref, polar_ref, *rest):
    fc, _, rows, n, _, per, count = dims
    if aliased:
        rest = rest[1:]
    predicted_ref = rest[0]
    returned = rest[1:-5]
    out_ref, turned_ref, all_ref, slot_ref, sems = rest[-5:]
    me = place_ref[1]
    for r in range(rows):
        slot_ref[r] = -1

    @pl.when(place_ref[3] > 0)
    def _():
        for c in range(CAP):
            slot_ref[polar_ref[place_ref[2] + c] - place_ref[0] * rows] = c
        for (t, lo, hi), piece in zip(plan.pieces(per, count), returned):
            all_ref[pl.ds((me ^ t) * per + lo, hi - lo)] = piece[plan.slot(t)]

    slots = [slot_ref[r] for r in range(rows)]

    def copy(f):
        return pltpu.make_async_copy(
            turned_ref.at[f], out_ref.at[f, pl.ds(group * SUB, SUB)], sems.at[f]
        )

    for f in range(fc):
        for lo in range(0, n, LANE):
            hi = min(lo + LANE, n)
            picked = []
            for r, slot in enumerate(slots):
                smooth = all_ref[jnp.maximum(slot, 0) * fc + f, :, lo:hi]
                picked.append(jnp.where(slot >= 0, smooth, predicted_ref[group, r, f, :, lo:hi]))
            turned_ref[f, :, :, lo:hi] = jnp.swapaxes(jnp.stack(picked), 0, 1)
        copy(f).start()
    for f in range(fc):
        copy(f).wait()


def merge(scalars, out, predicted, returned, group, plan, dims):
    fc, levels, rows, n, width, per, count = dims
    aliased = out is not None
    return pl.pallas_call(
        functools.partial(merge_kernel, dims, plan, group, aliased),
        in_specs=[whole(SMEM)] * 2 + [whole(pl.ANY)] * aliased + [whole(VMEM)] * (1 + len(returned)),
        out_specs=whole(pl.ANY),
        out_shape=shape(fc, levels, rows, n),
        scratch_shapes=[
            VMEM((fc, SUB, rows, n), F32),
            VMEM((count * per, SUB, width), F32),
            SMEM((rows,), jnp.int32),
            pltpu.SemaphoreType.DMA((fc,)),
        ],
        input_output_aliases={2: 0} if aliased else {},
        compiler_params=limit(8),
        cost_estimate=cost(fc * rows * SUB * width, 12 * fc * rows * SUB * width),
        name="merge",
    )(*scalars, *([out] if aliased else []), predicted, *returned)


def partner(piece, t, ends, lat_count, count):
    tiles = list(range(ends)) + list(range(lat_count - ends, lat_count))
    pairs = [(a * count + o, a * count + (o ^ t)) for a in tiles for o in range(count)]
    return lax.ppermute(piece, ("lat", "lon"), pairs)


def across(piece, t, ends, lat_count, count):
    near = [(a, a + ends) for a in range(ends)]
    near += [(lat_count - 1 - a, lat_count - 1 - a - ends) for a in range(ends)]
    pairs = [(a * count + o, b * count + (o ^ t)) for a, b in near for o in range(count)]
    return lax.ppermute(piece, ("lat", "lon"), pairs)


def home(piece, ends, lat_count, count):
    near = [(a, a + ends) for a in range(ends)]
    near += [(lat_count - 1 - a, lat_count - 1 - a - ends) for a in range(ends)]
    pairs = [(b * count + o, a * count + o) for a, b in near for o in range(count)]
    return lax.ppermute(piece, ("lat", "lon"), pairs)


def substep(fields, inv_cos, coupling_lon, coupling_lat, polar_rows, bands):
    fc, levels, rows, n = fields.shape
    lat_count, count = lax.axis_size("lat"), lax.axis_size("lon")
    ends = polar_rows.shape[0] // (2 * CAP)
    width = -(-(n + 2 * HALO) // LANE) * LANE
    per = -(-fc * CAP // count)
    dims = (fc, levels, rows, n, width, per, count)
    length = n * count

    tile, me = lax.axis_index("lat"), lax.axis_index("lon")
    south_end = tile >= lat_count - ends
    is_polar = (tile < ends) | south_end
    order = jnp.where(south_end, tile - (lat_count - 2 * ends), tile)
    start = jnp.where(is_polar, order * CAP, 0)
    place = jnp.stack([tile, me, start, is_polar.astype(jnp.int32)]).astype(jnp.int32)

    def ring(x, axis, shift, closed):
        size = lax.axis_size(axis)
        pairs = [(i, (i + shift) % size) for i in range(size) if closed or 0 <= i + shift < size]
        return lax.ppermute(x, axis, pairs)

    groups = levels // SUB
    place_of = (ends, lat_count, count)
    relayed = [3] if count == 4 and lat_count >= 4 * ends else []
    cuts = [(0, 2 * SUB), (2 * SUB, levels)] if levels > 2 * SUB else [(0, levels)]
    fields, place = lax.optimization_barrier((fields, place))
    turned, firsts, lasts, head, tail, band = turn(fields, dims, cuts)
    north, south = [], []
    for i in range(len(cuts)):
        north.append(ring(lasts[i], "lat", 1, False))
        south.append(ring(firsts[i], "lat", -1, False))
    before = ring(tail, "lon", 1, True)
    after = ring(head, "lon", -1, True)
    table = tables(dims, length)

    def exchange(parts, make, halved):
        plans, arrived, earlier = [], [], None
        for group in range(groups):
            plan = Plan(group, parts, count, relayed, earlier, group in halved)
            earlier = make(group, plan)
            got = list(earlier)
            for i, (t, lo, hi) in enumerate(plan.pieces(per, count)):
                if t in relayed and lo > 0:
                    got[i] = partner(got[i], t, *place_of)
                elif t in relayed:
                    middle = across(got[i], t, *place_of)
                    got[i] = home(middle, *place_of)
            plans.append(plan)
            arrived.append(got)
            if group == plan.part[-1]:
                for t in plan.direct:
                    moved = partner(earlier[t], t, *place_of)
                    for member in plan.part:
                        arrived[member][t] = moved
        return plans, arrived

    alone = tuple((g,) for g in range(groups))
    there, back = (THERE, BACK) if groups == 4 else (alone, alone)
    new = None

    def advance(owned, plan):
        nonlocal turned, new
        known = [i for i, (lo, hi) in enumerate(cuts) if lo <= owned[-1] * SUB]
        halos = (*(north[i] for i in known), *(south[i] for i in known))
        turned, new, *sends = stencil(
            (place, inv_cos, coupling_lon, coupling_lat, polar_rows),
            halos, cuts[: len(known)], before, after, band, turned, new, owned, plan, dims,
        )
        return sends

    def beside_poles(group, plan):
        made = advance([group], plan)
        if group % 2 == 1 or group == groups - 1:
            advance(list(range(group - group % 2, group + 1)), None)
        return made

    sources, pieces = exchange(there, beside_poles, ())

    def smooth(group, plan):
        return polar_filter(
            (place, bands), table, pieces[group], sources[group], plan, dims, length
        )

    plans, returned = exchange(back, smooth, (groups - 1,))
    out = None
    for group in range(groups):
        out = merge(
            (place, polar_rows), out, new, returned[group], group, plans[group], dims
        )
    return out


def solution(mesh):
    return jax.shard_map(
        substep,
        mesh=mesh,
        in_specs=(P(None, None, "lat", "lon"), P("lat"), P(), P(), P(), P()),
        out_specs=P(None, None, "lat", "lon"),
        check_vma=False,
    )
```

```python
import functools
import math

import jax
import jax.numpy as jnp
from jax import lax
from jax.experimental import pallas as pl
from jax.experimental.pallas import tpu as pltpu
from jax.sharding import PartitionSpec as P


KMAX = 1024
CAP = 14
SUB = 8
LANE = 128
HALO = 3
THERE = ((0, 1), (2, 3))
BACK = ((0, 1), (2,), (3,))


VMEM = pltpu.VMEM
SMEM = pltpu.SMEM
F32 = jnp.float32
BF16 = jnp.bfloat16


def whole(space):
    return pl.BlockSpec(memory_space=space)


def shape(*dims, dtype=F32):
    return jax.ShapeDtypeStruct(dims, dtype)


def cost(flops, moved):
    return pl.CostEstimate(flops=int(flops), bytes_accessed=int(moved), transcendentals=0)


def limit(mib):
    return pltpu.CompilerParams(vmem_limit_bytes=mib << 20)


def turn_kernel(dims, cuts, fields_ref, all_ref, *rest):
    fc, levels, rows, n, width, _, _ = dims
    k = len(cuts)
    firsts, lasts = rest[:k], rest[k : 2 * k]
    head_ref, tail_ref, band_ref, buf_ref, sems = rest[2 * k :]
    groups = levels // SUB
    final = (n - 1) // LANE * LANE
    lane = lax.broadcasted_iota(jnp.int32, (SUB, LANE), 1)

    def copy(g, f):
        return pltpu.make_async_copy(
            fields_ref.at[f, pl.ds(g * SUB, SUB)], buf_ref.at[g % 2, f], sems.at[g % 2, f]
        )

    for f in range(fc):
        copy(0, f).start()
    offset = lax.broadcasted_iota(jnp.int32, band_ref.shape, 0) - LANE
    offset = offset - lax.broadcasted_iota(jnp.int32, band_ref.shape, 1)
    far = jnp.abs(offset)
    size = jnp.where(far == 1, 45.0, jnp.where(far == 2, -9.0, jnp.where(far == 3, 1.0, 0.0)))
    band_ref[...] = jnp.where(offset > 0, size, -size).astype(BF16)
    for g in range(groups):
        at = slice(g * SUB, (g + 1) * SUB)
        piece = [i for i, (lo, hi) in enumerate(cuts) if lo <= g * SUB < hi][0]
        inner = slice(g * SUB - cuts[piece][0], (g + 1) * SUB - cuts[piece][0])
        if g + 1 < groups:
            for f in range(fc):
                copy(g + 1, f).start()

        def field(f, carry):
            copy(g, f).wait()
            for lo in range(0, n, LANE):
                hi = min(lo + LANE, n)
                x = jnp.swapaxes(buf_ref[g % 2, f, :, :, lo:hi], 0, 1)
                all_ref[f, HALO : HALO + rows, at, lo:hi] = x
                for r in range(HALO):
                    firsts[piece][f, r, inner, lo:hi] = x[r]
                    lasts[piece][f, r, inner, lo:hi] = x[rows - HALO + r]
            pad = jnp.zeros((SUB, width - n), F32)
            for r in range(rows):
                all_ref[f, r + HALO, at, n:] = pad
            for r in range(HALO):
                firsts[piece][f, r, inner, n:] = pad
                lasts[piece][f, r, inner, n:] = pad
            for out_ref, lo, by in ((head_ref, 0, 0), (tail_ref, final, n - HALO - final)):
                packed = jnp.zeros((SUB, LANE), F32)
                for r in range(rows):
                    turned = pltpu.roll(all_ref[f, r + HALO, at, lo : lo + LANE], (HALO * r - by) % LANE, 1)
                    mine = (lane >= HALO * r) & (lane < HALO * (r + 1))
                    packed = jnp.where(mine, turned, packed)
                out_ref[f, at] = packed
            return carry

        lax.fori_loop(0, fc, field, 0)


def turn(fields, dims, cuts):
    fc, levels, rows, n, width, _, _ = dims
    row_shapes = [shape(fc, HALO, hi - lo, width) for lo, hi in cuts]
    shapes = [shape(fc, rows + 2 * HALO, levels, width)] + row_shapes * 2 + [shape(fc, levels, LANE)] * 2
    wide = 2 * LANE if width % (2 * LANE) == 0 else LANE
    shapes.append(shape(wide + 2 * LANE, wide, dtype=BF16))
    made = pl.pallas_call(
        functools.partial(turn_kernel, dims, cuts),
        in_specs=[whole(pltpu.HBM)],
        out_specs=[whole(VMEM)] * len(shapes),
        out_shape=shapes,
        scratch_shapes=[
            VMEM((2, fc, SUB, rows, n), F32),
            pltpu.SemaphoreType.DMA((2, fc)),
        ],
        compiler_params=limit(7),
        cost_estimate=cost(0, 8 * fc * levels * rows * width),
        name="turn",
    )(pltpu.with_memory_space_constraint(fields, pltpu.HBM))
    k = len(cuts)
    return made[0], made[1 : 1 + k], made[1 + k : 1 + 2 * k], *made[-3:]


def stencil_kernel(dims, plan, owned, ready, cuts_of, place_ref, inv_cos_ref, lon_ref, lat_ref, polar_ref, *rest):
    fc, _, rows, _, _, per, _ = dims
    k = len(cuts_of)
    norths, souths = rest[:k], rest[k : 2 * k]
    before_ref, after_ref, band_ref = rest[2 * k : 2 * k + 3]
    aliased = plan.aliased if plan else 0
    q_ref, new_ref, *sends = rest[2 * k + 4 + ready + aliased : -4]

    @pl.when((place_ref[3] > 0) == (plan is not None))
    def _():
        for own in owned:
            piece = [i for i, (lo, hi) in enumerate(cuts_of) if lo <= own * SUB < hi][0]
            here = slice(own * SUB, (own + 1) * SUB)
            there = slice(own * SUB - cuts_of[piece][0], (own + 1) * SUB - cuts_of[piece][0])
            for f in range(fc):
                for r in range(HALO):
                    q_ref[f, r, here] = norths[piece][f, r, there]
                    q_ref[f, rows + HALO + r, here] = souths[piece][f, r, there]

        def one(group, carry):
            predict(
                dims, group, inv_cos_ref, lon_ref, lat_ref, before_ref, after_ref, band_ref,
                q_ref, new_ref, *rest[-4:],
            )
            return carry

        lax.fori_loop(owned[0], owned[-1] + 1, one, 0)
        me = place_ref[1]
        unit = 3 if per % 3 == 0 and fc % 3 == 0 else 1
        for t, send in enumerate(sends):

            def pick(k, carry):
                p = jnp.minimum((me ^ t) * per + unit * k, fc * CAP - unit)
                c = lax.div(p, fc)
                r = polar_ref[place_ref[2] + c] - place_ref[0] * rows
                some = new_ref[owned[0], r, pl.ds(p - c * fc, unit)]
                send[plan.slot(t), pl.ds(unit * k, unit)] = some
                return carry

            lax.fori_loop(0, per // unit, pick, 0)


def predict(
    dims, group, inv_cos_ref, lon_ref, lat_ref, before_ref, after_ref, band_ref,
    q_ref, new_ref, factor_ref, high_ref, low_ref, dlon_ref,
):
    fc, _, rows, n, width, _, _ = dims
    off = n % LANE
    lane = lax.broadcasted_iota(jnp.int32, (SUB, LANE), 1)
    at = pl.ds(pl.multiple_of(group * SUB, SUB), SUB)
    tiles = width // LANE
    cuts = [slice(i * LANE, (i + 1) * LANE) for i in range(tiles)]
    for f in range(fc):
        for k in range(fc):
            factor_ref[0, f, k] = jnp.full((SUB, LANE), lon_ref[f, k] * (1.0 / 60.0), F32)
            factor_ref[1, f, k] = jnp.full((SUB, LANE), lat_ref[f, k] * (1.0 / 60.0), F32)

    def lay(r2, carry):
        for f in range(fc):
            base = pl.multiple_of((f * rows + 2 * r2) * SUB, 2 * SUB)
            after, before = after_ref[f, at], before_ref[f, at]
            for i in range(tiles):
                x = q_ref[f, pl.ds(HALO + 2 * r2, 2), at, cuts[i]]
                if i == tiles - 1:
                    edge = []
                    for k in range(2):
                        shift = HALO * (2 * r2 + k)
                        right = pltpu.roll(after, lax.rem(off + HALO * LANE - shift, LANE), 1)
                        left = pltpu.roll(before, LANE - HALO - shift, 1)
                        edge.append(jnp.where(lane < off + HALO, right, left))
                    x = jnp.where((lane < off)[None], x, jnp.stack(edge))
                high, low = split(x.reshape(2 * SUB, LANE))
                for spot in [i + 1] + [0] * (i == tiles - 1) + [tiles + 1] * (i == 0):
                    cut = slice(spot * LANE, (spot + 1) * LANE)
                    high_ref[pl.ds(base, 2 * SUB), cut] = high
                    low_ref[pl.ds(base, 2 * SUB), cut] = low
        return carry

    lax.fori_loop(0, rows // 2, lay, 0)
    wide = band_ref.shape[1]
    for lo in range(0, width, wide):
        window = slice(lo, lo + wide + 2 * LANE)
        dot = functools.partial(jnp.dot, preferred_element_type=F32)
        both = dot(high_ref[:, window], band_ref[...]) + dot(low_ref[:, window], band_ref[...])
        dlon_ref[:, lo : lo + wide] = both

    def row(r, carry):
        scale = inv_cos_ref[r]
        for cut in cuts:
            dlon, dlat = [], []
            for f in range(fc):
                spot = pl.multiple_of((f * rows + r) * SUB, SUB)
                dlon.append(dlon_ref[pl.ds(spot, SUB), cut] * scale)
                q = lambda o: q_ref[f, r + HALO + o, at, cut]
                dlat.append(45.0 * (q(1) - q(-1)) - 9.0 * (q(2) - q(-2)) + (q(3) - q(-3)))
            for f in range(fc):
                acc = q_ref[f, r + HALO, at, cut]
                for k in range(fc):
                    acc = acc + (factor_ref[0, f, k] * dlon[k] + factor_ref[1, f, k] * dlat[k])
                new_ref[group, r, f, :, cut] = acc
        return carry

    lax.fori_loop(0, rows, row, 0)


class Plan:
    def __init__(self, group, parts, count, relayed, earlier, halved=False):
        self.halved = relayed if halved else []
        part = [p for p in parts if group in p][0]
        self.size = len(part)
        self.inside = part.index(group)
        self.part = part
        self.direct = [t for t in range(1, count) if t not in relayed]
        self.earlier = [earlier[t] for t in self.direct] if self.inside else []
        self.aliased = len(self.earlier)

    def slot(self, t):
        return self.inside if t in self.direct else 0

    def pieces(self, per, count):
        found = []
        for t in range(count):
            stops = (5 * per // 8, per) if t in self.halved else (per,)
            found += [(t, lo, hi) for lo, hi in zip((0, *stops), stops)]
        return found

    def shapes(self, dims):
        _, _, _, _, width, per, count = dims
        return [
            shape(self.size if t in self.direct else 1, hi - lo, SUB, width)
            for t, lo, hi in self.pieces(per, count)
        ]

    def aliases(self, first_in, first_out, per, count):
        if not self.aliased:
            return {}
        at = [t for t, _, _ in self.pieces(per, count)]
        return {first_in + i: first_out + at.index(t) for i, t in enumerate(self.direct)}


def stencil(scalars, halos, cuts, before, after, band, turned, new, owned, plan, dims):
    fc, levels, rows, _, width, per, count = dims
    groups = levels // SUB
    sends = plan.shapes(dims) if plan else []
    earlier = plan.earlier if plan else []
    arrays = [*halos, before, after, band, turned]
    first = len(scalars) + len(arrays)
    aliases = {first - 1: 0}
    ready = new is not None
    if ready:
        arrays.append(new)
        aliases[first] = 1
    if plan:
        aliases.update(plan.aliases(first + ready, 2, per, count))
    return pl.pallas_call(
        functools.partial(stencil_kernel, dims, plan, owned, ready, cuts),
        in_specs=[whole(SMEM)] * 5 + [whole(VMEM)] * (len(arrays) + len(earlier)),
        out_specs=[whole(VMEM)] * (2 + len(sends)),
        out_shape=[shape(*turned.shape), shape(groups, rows, fc, SUB, width)] + sends,
        scratch_shapes=[
            VMEM((2, fc, fc, SUB, LANE), F32),
            VMEM((fc * rows * SUB, width + 2 * LANE), BF16),
            VMEM((fc * rows * SUB, width + 2 * LANE), BF16),
            VMEM((fc * rows * SUB, width), F32),
        ],
        input_output_aliases=aliases,
        compiler_params=limit(8),
        cost_estimate=cost(100 * fc * rows * SUB * width, 12 * fc * rows * SUB * width),
        name="stencil",
    )(*scalars, *arrays, *earlier)


def table_kernel(dims, length, high_ref, low_ref, base_ref, step_ref):
    _, _, _, n, width, _, count = dims
    parts = count // 4
    quarter = KMAX // 4
    step = 32
    column = lax.broadcasted_iota(jnp.int32, (1, KMAX), 1)
    block = column // quarter
    residue = jnp.where(block == 1, 2, jnp.where(block == 2, 1, block))
    wave = 4 * (column - block * quarter) + residue

    def circle(cell):
        number = (cell * wave).astype(F32)
        turns = jnp.floor(number * (1.0 / length))
        phase = (number - turns * length) * (2.0 * math.pi / length)
        return jnp.cos(phase), jnp.sin(phase)

    c2, s2 = circle(lax.broadcasted_iota(jnp.int32, (step, KMAX), 0))
    step_ref[0], step_ref[1] = c2, s2
    blocks = width // step
    for s in range(parts):
        c1, s1 = circle(step * lax.broadcasted_iota(jnp.int32, (blocks, KMAX), 0) + s * n)
        base_ref[0], base_ref[1] = c1, s1

        def band(a, carry):
            c1, s1 = base_ref[0, pl.ds(a, 1), :], base_ref[1, pl.ds(a, 1), :]
            inside = a * step + lax.broadcasted_iota(jnp.int32, (step, quarter), 0) < n
            at = pl.ds(pl.multiple_of(s * width + a * step, step), step)
            for i in range(4):
                cut = slice(i * quarter, (i + 1) * quarter)
                c2, s2 = step_ref[0, :, cut], step_ref[1, :, cut]
                cosine = c1[:, cut] * c2 - s1[:, cut] * s2
                sine = s1[:, cut] * c2 + c1[:, cut] * s2
                for value, col in ((cosine, (0, 2, 4, 5)[i]), (sine, (1, 3, 6, 7)[i])):
                    value = jnp.where(inside, value, 0.0)
                    high, low = split(value)
                    out = slice(col * quarter, (col + 1) * quarter)
                    high_ref[at, out] = high
                    low_ref[at, out] = low
            return carry

        lax.fori_loop(0, blocks, band, 0)


def tables(dims, length):
    _, _, _, _, width, _, count = dims
    out = shape(count // 4 * width, 2 * KMAX, dtype=BF16)
    return pl.pallas_call(
        functools.partial(table_kernel, dims, length),
        out_specs=[whole(VMEM)] * 2,
        out_shape=[out] * 2,
        scratch_shapes=[VMEM((2, width // 32, KMAX), F32), VMEM((2, 32, KMAX), F32)],
        compiler_params=limit(4),
        cost_estimate=cost(20 * count // 4 * width * 2 * KMAX, 4 * count // 4 * width * 2 * KMAX),
        name="tables",
    )()


def split(x):
    high = x.astype(BF16)
    return high, (x - high.astype(F32)).astype(BF16)


def product(left, high, low, turned):
    half = left.shape[0] // 2
    dims = (((1,), (1 if turned else 0,)), ((), ()))
    dot = lambda x, y: lax.dot_general(x, y, dims, preferred_element_type=F32)
    both = dot(left, high)
    return both[:half] + (both[half:] + dot(left[:half], low))


def by_partner(pieces, me):
    count = len(pieces)
    bit = 1
    while bit < count:
        flag = (me & bit) > 0
        pieces = [jnp.where(flag, pieces[i ^ bit], pieces[i]) for i in range(count)]
        bit *= 2
    return pieces


def filter_kernel(dims, source, plan, length, place_ref, bands_ref, high_ref, low_ref, *rest):
    fc, _, _, _, width, per, count = dims
    inputs, outputs = rest[:count], rest[count + plan.aliased : -3]
    left_ref, spec_ref, band_ref = rest[-3:]
    me = place_ref[1]
    parts = count // 4
    m = per * SUB
    quarter = KMAX // 4

    @pl.when(place_ref[3] > 0)
    def _():
        for p in range(count * per):
            c = min(p // fc, CAP - 1)
            band_ref[p * SUB : (p + 1) * SUB] = jnp.full(
                (SUB, LANE), bands_ref[place_ref[2] + c], jnp.int32
            )
        mine = pl.ds(pl.multiple_of(me * m, SUB), m)
        band = jnp.concatenate([band_ref[mine]] * (quarter // LANE), axis=1)
        waves = 4 * lax.broadcasted_iota(jnp.int32, (m, quarter), 1)

        def weight(residue):
            k = waves + residue
            factor = jnp.where(k == 0, 1.0 / length, 2.0 / length)
            return jnp.where(k < band, factor, 0.0)

        def spot(i, term):
            return (2 * i + term) * m if i < 2 else (4 + (i - 2) + 2 * term) * m

        def keep(i, col, value):
            for term, x in enumerate(split(value)):
                spec_ref[spot(i, term) : spot(i, term) + m, col * quarter : (col + 1) * quarter] = x

        for lo in range(0, width, LANE):
            lanes = slice(lo, lo + LANE)
            x = by_partner(
                [ref[source.slot(t), :, :, lanes].reshape(m, LANE) for t, ref in enumerate(inputs)], me
            )
            for s in range(parts):
                x0, x1, x2, x3 = (x[i * parts + s] for i in range(4))
                e0, e1 = x0 + x2, x1 + x3
                cut = slice(s * width + lo, s * width + lo + LANE)
                for i, y in enumerate((e0 + e1, e0 - e1, x0 - x2, x1 - x3)):
                    for term, z in enumerate(split(y)):
                        left_ref[spot(i, term) : spot(i, term) + m, cut] = z

        for i in range(2):
            w = weight(2 * i)
            for c in range(2):
                cols = slice((2 * i + c) * quarter, (2 * i + c + 1) * quarter)
                left = left_ref[2 * m * i : 2 * m * (i + 1)]
                keep(i, c, product(left, high_ref[:, cols], low_ref[:, cols], False) * w)

        def forward(col):
            cols = slice(col * quarter, (col + 1) * quarter)
            return product(left_ref[4 * m :], high_ref[:, cols], low_ref[:, cols], False)

        for i in range(2):
            w = weight(2 * i + 1)
            cosine, sine = forward(4 + i), forward(6 + i)
            if i == 0:
                c = (cosine[:m] - sine[m:]) * w
                s = (sine[:m] + cosine[m:]) * w
            else:
                c = (cosine[:m] + sine[m:]) * w
                s = (sine[:m] - cosine[m:]) * w
            keep(2, i, c)
            keep(2, 2 + i, s)
            keep(3, i, s if i == 0 else -s)
            keep(3, 2 + i, -c if i == 0 else c)

        wide = 2 * LANE if width % (2 * LANE) == 0 else LANE

        def inverse(rows_at, terms, col, cells):
            cols = slice(col * quarter, (col + terms) * quarter)
            left = spec_ref[rows_at, : terms * quarter]
            return product(left, high_ref[cells, cols], low_ref[cells, cols], True)

        def block(j, carry):
            lanes = pl.ds(pl.multiple_of(j * wide, wide), wide)
            pieces = [None] * count
            for s in range(parts):
                cells = pl.ds(pl.multiple_of(s * width + j * wide, wide), wide)
                whole_part = inverse(slice(0, 2 * m), 2, 0, cells)
                half = inverse(slice(2 * m, 4 * m), 2, 2, cells)
                odd = inverse(slice(4 * m, 8 * m), 4, 4, cells)
                o0, o1 = odd[:m], odd[m:]
                p, d = whole_part + half, whole_part - half
                for i, y in enumerate((p + o0, d + o1, p - o0, d - o1)):
                    pieces[i * parts + s] = y
            found = by_partner(pieces, me)
            for (t, lo, hi), out_ref in zip(plan.pieces(per, count), outputs):
                y = found[t][lo * SUB : hi * SUB].reshape(hi - lo, SUB, wide)
                out_ref[plan.slot(t), :, :, lanes] = y
            return carry

        lax.fori_loop(0, width // wide, block, 0)


def polar_filter(scalars, table, pieces, source, plan, dims, length):
    _, _, _, _, width, per, count = dims
    m = per * SUB
    parts = count // 4
    return pl.pallas_call(
        functools.partial(filter_kernel, dims, source, plan, length),
        in_specs=[whole(SMEM)] * 2 + [whole(VMEM)] * (2 + count + plan.aliased),
        out_specs=[whole(VMEM)] * len(plan.shapes(dims)),
        out_shape=plan.shapes(dims),
        scratch_shapes=[
            VMEM((8 * m, parts * width), BF16),
            VMEM((8 * m, KMAX), BF16),
            VMEM((count * m, LANE), jnp.int32),
        ],
        input_output_aliases=plan.aliases(4 + count, 0, per, count),
        compiler_params=limit(10),
        cost_estimate=cost(18 * m * width * parts * 4 * KMAX, 8 * count * m * width),
        name="polar_filter",
    )(*scalars, *table, *pieces, *plan.earlier)


def merge_kernel(dims, plan, group, aliased, place_ref, polar_ref, *rest):
    fc, _, rows, n, _, per, count = dims
    if aliased:
        rest = rest[1:]
    predicted_ref = rest[0]
    returned = rest[1:-5]
    out_ref, turned_ref, all_ref, slot_ref, sems = rest[-5:]
    me = place_ref[1]
    for r in range(rows):
        slot_ref[r] = -1

    @pl.when(place_ref[3] > 0)
    def _():
        for c in range(CAP):
            slot_ref[polar_ref[place_ref[2] + c] - place_ref[0] * rows] = c
        for (t, lo, hi), piece in zip(plan.pieces(per, count), returned):
            all_ref[pl.ds((me ^ t) * per + lo, hi - lo)] = piece[plan.slot(t)]

    slots = [slot_ref[r] for r in range(rows)]

    def copy(f):
        return pltpu.make_async_copy(
            turned_ref.at[f], out_ref.at[f, pl.ds(group * SUB, SUB)], sems.at[f]
        )

    for f in range(fc):
        for lo in range(0, n, LANE):
            hi = min(lo + LANE, n)
            picked = []
            for r, slot in enumerate(slots):
                smooth = all_ref[jnp.maximum(slot, 0) * fc + f, :, lo:hi]
                picked.append(jnp.where(slot >= 0, smooth, predicted_ref[group, r, f, :, lo:hi]))
            turned_ref[f, :, :, lo:hi] = jnp.swapaxes(jnp.stack(picked), 0, 1)
        copy(f).start()
    for f in range(fc):
        copy(f).wait()


def merge(scalars, out, predicted, returned, group, plan, dims):
    fc, levels, rows, n, width, per, count = dims
    aliased = out is not None
    return pl.pallas_call(
        functools.partial(merge_kernel, dims, plan, group, aliased),
        in_specs=[whole(SMEM)] * 2 + [whole(pl.ANY)] * aliased + [whole(VMEM)] * (1 + len(returned)),
        out_specs=whole(pl.ANY),
        out_shape=shape(fc, levels, rows, n),
        scratch_shapes=[
            VMEM((fc, SUB, rows, n), F32),
            VMEM((count * per, SUB, width), F32),
            SMEM((rows,), jnp.int32),
            pltpu.SemaphoreType.DMA((fc,)),
        ],
        input_output_aliases={2: 0} if aliased else {},
        compiler_params=limit(6),
        cost_estimate=cost(fc * rows * SUB * width, 12 * fc * rows * SUB * width),
        name="merge",
    )(*scalars, *([out] if aliased else []), predicted, *returned)


def partner(piece, t, ends, lat_count, count):
    tiles = list(range(ends)) + list(range(lat_count - ends, lat_count))
    pairs = [(a * count + o, a * count + (o ^ t)) for a in tiles for o in range(count)]
    return lax.ppermute(piece, ("lat", "lon"), pairs)


def across(piece, t, ends, lat_count, count):
    near = [(a, a + ends) for a in range(ends)]
    near += [(lat_count - 1 - a, lat_count - 1 - a - ends) for a in range(ends)]
    pairs = [(a * count + o, b * count + (o ^ t)) for a, b in near for o in range(count)]
    return lax.ppermute(piece, ("lat", "lon"), pairs)


def home(piece, ends, lat_count, count):
    near = [(a, a + ends) for a in range(ends)]
    near += [(lat_count - 1 - a, lat_count - 1 - a - ends) for a in range(ends)]
    pairs = [(b * count + o, a * count + o) for a, b in near for o in range(count)]
    return lax.ppermute(piece, ("lat", "lon"), pairs)


def substep(fields, inv_cos, coupling_lon, coupling_lat, polar_rows, bands):
    fc, levels, rows, n = fields.shape
    lat_count, count = lax.axis_size("lat"), lax.axis_size("lon")
    ends = polar_rows.shape[0] // (2 * CAP)
    width = -(-(n + 2 * HALO) // LANE) * LANE
    per = -(-fc * CAP // count)
    dims = (fc, levels, rows, n, width, per, count)
    length = n * count

    tile, me = lax.axis_index("lat"), lax.axis_index("lon")
    south_end = tile >= lat_count - ends
    is_polar = (tile < ends) | south_end
    order = jnp.where(south_end, tile - (lat_count - 2 * ends), tile)
    start = jnp.where(is_polar, order * CAP, 0)
    place = jnp.stack([tile, me, start, is_polar.astype(jnp.int32)]).astype(jnp.int32)

    def ring(x, axis, shift, closed):
        size = lax.axis_size(axis)
        pairs = [(i, (i + shift) % size) for i in range(size) if closed or 0 <= i + shift < size]
        return lax.ppermute(x, axis, pairs)

    groups = levels // SUB
    place_of = (ends, lat_count, count)
    relayed = [3] if count == 4 and lat_count >= 4 * ends else []
    cuts = [(0, 2 * SUB), (2 * SUB, levels)] if levels > 2 * SUB else [(0, levels)]
    fields, place = lax.optimization_barrier((fields, place))
    turned, firsts, lasts, head, tail, band = turn(fields, dims, cuts)
    north, south = [], []
    for i in range(len(cuts)):
        north.append(ring(lasts[i], "lat", 1, False))
        south.append(ring(firsts[i], "lat", -1, False))
    before = ring(tail, "lon", 1, True)
    after = ring(head, "lon", -1, True)
    table = tables(dims, length)

    def exchange(parts, make, halved):
        plans, arrived, earlier = [], [], None
        for group in range(groups):
            plan = Plan(group, parts, count, relayed, earlier, group in halved)
            earlier = make(group, plan)
            got = list(earlier)
            for i, (t, lo, hi) in enumerate(plan.pieces(per, count)):
                if t in relayed and lo > 0:
                    got[i] = partner(got[i], t, *place_of)
                elif t in relayed:
                    middle = across(got[i], t, *place_of)
                    got[i] = home(middle, *place_of)
            plans.append(plan)
            arrived.append(got)
            if group == plan.part[-1]:
                for t in plan.direct:
                    moved = partner(earlier[t], t, *place_of)
                    for member in plan.part:
                        arrived[member][t] = moved
        return plans, arrived

    alone = tuple((g,) for g in range(groups))
    there, back = (THERE, BACK) if groups == 4 else (alone, alone)
    new = None

    def advance(owned, plan):
        nonlocal turned, new
        known = [i for i, (lo, hi) in enumerate(cuts) if lo <= owned[-1] * SUB]
        halos = (*(north[i] for i in known), *(south[i] for i in known))
        turned, new, *sends = stencil(
            (place, inv_cos, coupling_lon, coupling_lat, polar_rows),
            halos, cuts[: len(known)], before, after, band, turned, new, owned, plan, dims,
        )
        return sends

    def beside_poles(group, plan):
        made = advance([group], plan)
        if group % 2 == 1 or group == groups - 1:
            advance(list(range(group - group % 2, group + 1)), None)
        return made

    sources, pieces = exchange(there, beside_poles, ())

    def smooth(group, plan):
        return polar_filter(
            (place, bands), table, pieces[group], sources[group], plan, dims, length
        )

    plans, returned = exchange(back, smooth, (groups - 1,))
    out = None
    for group in range(groups):
        out = merge(
            (place, polar_rows), out, new, returned[group], group, plans[group], dims
        )
    return out


def solution(mesh):
    return jax.shard_map(
        substep,
        mesh=mesh,
        in_specs=(P(None, None, "lat", "lon"), P("lat"), P(), P(), P(), P()),
        out_specs=P(None, None, "lat", "lon"),
        check_vma=False,
    )
```
